256 devices in a mesh: fib: 32 (over y, z), wav: 4 (over x), exp: 2 (over core).
Axes of the slice: x: 4, y: 4, z: 8, core: 2. Of those that a mesh axis runs over, the one named last changes fastest.
Arguments:
- pixels: float32 [8, 1920, 8192], P('exp', 'wav', 'fib'), may hold values from -6 to 6
- pixel_ivar: float32 [8, 1920, 8192], P('exp', 'wav', 'fib'), may hold values from 0.25 to 4
- clip_bits: int32 [8, 128, 8192], P('exp', 'wav', 'fib'), may hold values from 0 to 32767
- coupling: float32 [8192], P('fib'), may hold values from 0.5 to 200
- counts: int32 [8192], P('fib'), may hold values from 1 to 8
- good_flags: int32 [8, 8192], P('exp', 'fib'), may hold values 0 or 1
- owner_slot: int32 [8192], replicated, may hold values from 0 to 8191, as said below
Outputs:
- coadd_flux: float32 [1920, 8192], P(('wav', 'exp'), 'fib')
- coadd_ivar: float32 [1920, 8192], P(('wav', 'exp'), 'fib')
- coadd_res: float32 [3, 1920, 8192], P(None, ('wav', 'exp'), 'fib')
The draws below stay inside these ranges and needn't reach their ends.
Inputs may be any that keep to these rules, and one draw needn't show every extreme that they name: A permutation of the fibres; fibre f belongs to coadd index owner_slot[f] // 256 of fib, and the 256 fibres of each index of fib go 8 to every coadd index.
All inputs are finite; a program needn't handle non-finite values. No bound on the sum of `good_flags` on one device may be relied on, other than what follows from the above.
Results may differ from the reference program's by a relative error of at most 0.0001.
Values sent between devices are 32-bit elements; how exact they have to be, the bound alone decides.
A program may use at most 128 MiB of HBM per device.

```python
import math
import jax
import jax.numpy as jnp
from jax import lax

F_DEV = 256
HALO = 50
FIBRES = 8192
EXPOS = 8
WAVES = 1920
N_WAV = 4


def draw_clip_bits(key, part):
    kept_pixels = (jax.random.randint(key, (EXPOS, WAVES // 15, 15, FIBRES), 0, 8) != 0).astype(jnp.int32)
    shifts = jnp.arange(15, dtype=jnp.int32)
    return jnp.sum(kept_pixels << shifts[None, None, :, None], axis=2).astype(jnp.int32)


def shuffle_slots(one_key):
    return jax.random.permutation(one_key, F_DEV)


def shuffle_row(one_key, row_values):
    return jax.random.permutation(one_key, row_values)


def draw_owner_slot(key, part):
    owners = FIBRES // F_DEV
    per_owner = F_DEV // owners
    source = jnp.arange(owners, dtype=jnp.int32)[:, None, None]
    target = jnp.arange(owners, dtype=jnp.int32)[None, :, None]
    offset = jnp.arange(per_owner, dtype=jnp.int32)[None, None, :]
    within = source * per_owner + offset + target * 0
    target_full = target + source * 0 + offset * 0
    target_keys = jax.random.split(jax.random.fold_in(key, 11), owners)
    target_perms = jax.vmap(shuffle_slots)(target_keys).astype(jnp.int32)
    slots = target_full * F_DEV + target_perms[target_full, within]
    rows_all = slots.reshape(owners, F_DEV)
    source_keys = jax.random.split(jax.random.fold_in(key, 12), owners)
    rows_all = jax.vmap(shuffle_row)(source_keys, rows_all)
    return rows_all.reshape(-1).astype(jnp.int32)


def touch_ends(values, key, smallest, largest):
    dims = values.shape
    index_at = [jax.random.randint(jax.random.fold_in(key, axis), (), 0, dims[axis]) for axis in range(len(dims))]
    values = values.at[tuple(index_at)].set(smallest)
    longest = dims.index(max(dims))
    index_at[longest] = (index_at[longest] + 1) % dims[longest]
    return values.at[tuple(index_at)].set(largest)


def levels(rng, extent, cuts, low, largest):
    factor_of = 1.0
    for axis_at, parts in cuts:
        steps = jax.random.uniform(jax.random.fold_in(jax.random.fold_in(rng, 6), axis_at), (parts,), jnp.float32, low / len(cuts), largest / len(cuts))
        factor_of = factor_of * jnp.repeat(jnp.exp(steps), extent[axis_at] // parts).reshape((-1,) + (1,) * (len(extent) - 1 - axis_at))
    return factor_of


def centred(key, shape, scale, reach, pieces=(), held_as=jnp.bfloat16):
    entries = jax.random.normal(key, shape, jnp.float32) * scale
    if len(pieces) > 0:
        entries = levels(key, shape, pieces, -0.22, 0.18) * entries
    return jnp.clip(entries, min=-reach, max=reach).astype(held_as)


def setup_inputs(seed: int = 0) -> dict:
    key_of = jax.random.split(jax.random.key(seed), 8)
    pixels = centred(key_of[0], (EXPOS, WAVES, FIBRES), 1.0, 6.0, ((0, 2), (1, 4), (2, 32)), jnp.float32)
    pixel_ivar = jnp.clip(jnp.exp(math.log(4.0) - 2.7725887 * jax.random.uniform(key_of[1], (EXPOS, WAVES, FIBRES), jnp.float32) ** levels(key_of[1], (EXPOS, WAVES, FIBRES), ((0, 2), (1, 4), (2, 32)), -0.2, 0.2)), 0.25, 4.0)
    clip_bits = draw_clip_bits(jax.random.fold_in(key_of[7], 71), 0)
    coupling = jnp.clip(jnp.exp(math.log(200.0) - 5.9914645 * jax.random.uniform(key_of[3], (FIBRES,), jnp.float32) ** levels(key_of[3], (FIBRES,), ((0, 32),), -0.2, 0.2)), 0.5, 200.0)
    counts = touch_ends(jax.random.randint(key_of[4], (FIBRES,), 1, EXPOS + 1), jax.random.fold_in(key_of[4], 1), 1, EXPOS).astype(jnp.int32)
    good_flags = touch_ends((jax.random.randint(key_of[5], (EXPOS, FIBRES), 0, 8) < 7).astype(jnp.int32), jax.random.fold_in(key_of[5], 1), 0, 1)
    owner_slot = draw_owner_slot(jax.random.fold_in(key_of[7], 71), 0)
    return {"pixels": pixels, "pixel_ivar": pixel_ivar, "clip_bits": clip_bits, "coupling": coupling, "counts": counts, "good_flags": good_flags, "owner_slot": owner_slot}


def reference(pixels, pixel_ivar, clip_bits, coupling, counts, good_flags, owner_slot):
    expos, waves, fibres = pixels.shape
    patch_width = waves // N_WAV
    length = patch_width + 2 * HALO
    padding = ((0, 0), (HALO, HALO), (0, 0))
    pad_pixels = jnp.pad(pixels, padding)
    pad_ivar = jnp.pad(pixel_ivar, padding)
    flux_parts = []
    band_parts = []
    for patch_index in range(N_WAV):
        start = patch_index * patch_width
        window_pixels = pad_pixels[:, start:start + length]
        window_ivar = pad_ivar[:, start:start + length]
        position = start - HALO + jnp.arange(length, dtype=jnp.int32)
        inside = ((position >= 0) & (position < waves)).astype(jnp.float32)
        linkage = coupling[None, :] * (inside[:-1] * inside[1:])[:, None]
        border = jnp.zeros((1, fibres), jnp.float32)
        link_left = jnp.concatenate([border, linkage], 0)[None]
        link_right = jnp.concatenate([linkage, border], 0)[None]
        middle = window_ivar * inside[None, :, None] + (1.0 - inside)[None, :, None] + link_left + link_right
        weighted = window_ivar * window_pixels
        lower_band = jnp.broadcast_to(-link_left, middle.shape)
        upper_band = jnp.broadcast_to(-link_right, middle.shape)
        solved = lax.linalg.tridiagonal_solve(jnp.transpose(lower_band, (0, 2, 1)), jnp.transpose(middle, (0, 2, 1)), jnp.transpose(upper_band, (0, 2, 1)), jnp.transpose(weighted, (0, 2, 1))[..., None])[..., 0]
        solved = jnp.transpose(solved, (0, 2, 1))
        flux_parts.append(solved[:, HALO:HALO + patch_width])
        row_total = middle + link_left + link_right
        bands = jnp.stack([link_left / row_total, middle / row_total, link_right / row_total])
        band_parts.append(bands[:, :, HALO:HALO + patch_width])
    flux = jnp.concatenate(flux_parts, 1)
    resolution = jnp.concatenate(band_parts, 2)
    shifts = jnp.arange(15, dtype=jnp.int32)
    kept_pixels = (clip_bits[:, :, None, :] >> shifts[None, None, :, None] & 1).reshape(expos, waves, fibres).astype(jnp.float32)
    exposure = jnp.arange(expos, dtype=jnp.int32)
    usable = good_flags.astype(jnp.float32) * (exposure[:, None] < counts[None, :]).astype(jnp.float32)
    weight = pixel_ivar * kept_pixels * usable[:, None, :]
    flux_sum = jnp.sum(weight * flux, 0)
    weight_sum = jnp.sum(weight, 0)
    band_sum = jnp.sum(weight[None] * resolution, 1)
    divisor = jnp.maximum(weight_sum, 1.0)
    inverse = jnp.argsort(owner_slot)
    coadd_flux = (flux_sum / divisor)[:, inverse]
    coadd_ivar = weight_sum[:, inverse]
    coadd_res = (band_sum / divisor[None])[:, :, inverse]
    return (coadd_flux, coadd_ivar, coadd_res)
```

```python
import functools

import jax
import jax.numpy as jnp
from jax import lax
from jax.experimental import pallas as pl
from jax.experimental.pallas import tpu as pltpu
from jax.sharding import PartitionSpec as P

HALO = 50
BLOCKS = 8
BITS = 15
LANES = 128
HALVES = 2
F_DEV = LANES * HALVES
ROWS = 256
SLOT_ROW = 240

F32 = jnp.float32
BF16 = jnp.bfloat16


def pieces(x):
    high = x.astype(BF16)
    rest = x - high.astype(F32)
    middle = rest.astype(BF16)
    low = (rest - middle.astype(F32)).astype(BF16)
    return high, middle, low


def exact_dot(one_hot, x, dims, one_hot_first):
    total = None
    for piece in pieces(x):
        pair = (one_hot, piece) if one_hot_first else (piece, one_hot)
        part = lax.dot_general(*pair, (dims, ((), ())), preferred_element_type=F32)
        total = part if total is None else total + part
    return total


def exchange_kernel(
    n_fib,
    n_wav,
    pix_hbm,
    ivar_hbm,
    bits_hbm,
    coupling_ref,
    counts_ref,
    good_ref,
    slots_ref,
    got_a,
    got_b,
    pix,
    ivar,
    bits,
    weight,
    fac_m,
    fac_y,
    fac_q,
    sums,
    theirs,
    send_a,
    send_b,
    sort_ref,
    edge_out,
    edge_in,
    red,
    far,
    load_sem,
    edge_send,
    edge_recv,
    half_send,
    half_recv,
    a_send,
    a_recv,
    b_send,
    b_recv,
):
    fib, wav, exp = lax.axis_index("fib"), lax.axis_index("wav"), lax.axis_index("exp")
    e_dev = good_ref.shape[0]
    chains = e_dev * HALVES
    waves = ivar.shape[1]
    step_count = waves // BLOCKS
    words = bits.shape[1] // BLOCKS
    half = waves // 2
    per = F_DEV // n_fib

    loads = []

    def load(src, dst, rows, number):
        for chain in range(chains):
            e, h = chain // HALVES, chain % HALVES
            copy = pltpu.make_async_copy(
                src.at[e, :, pl.ds(h * LANES, LANES)], dst.at[chain], load_sem.at[number, chain]
            )
            copy.start()
            loads.append(copy)

    load(bits_hbm, bits, None, 0)
    load(ivar_hbm, ivar, None, 1)
    load(pix_hbm, pix, None, 2)

    def to(**where):
        return {"device_id": where, "device_id_type": pl.DeviceIdType.MESH}

    def fib_peer(k):
        return lax.rem(fib + k, n_fib)

    wav_right = lax.rem(wav + 1, n_wav)
    wav_left = lax.rem(wav + n_wav - 1, n_wav)
    partner = 1 - exp

    barrier = pltpu.get_barrier_semaphore()

    def greet(k, _):
        pl.semaphore_signal(barrier, inc=1, **to(fib=fib_peer(k)))
        return 0

    pl.semaphore_signal(barrier, inc=1, **to(exp=partner))
    pl.semaphore_signal(barrier, inc=1, **to(wav=wav_right))
    pl.semaphore_signal(barrier, inc=1, **to(wav=wav_left))
    lax.fori_loop(1, n_fib, greet, 0)

    slot_row = jnp.concatenate(
        [slots_ref[pl.ds(fib * HALVES + h, 1), :] for h in range(HALVES)], axis=1
    )
    owner = slot_row // F_DEV
    owned = owner == lax.broadcasted_iota(jnp.int32, (n_fib, F_DEV), 0)
    before = lax.broadcasted_iota(jnp.int32, (F_DEV, F_DEV), 0) < lax.broadcasted_iota(
        jnp.int32, (F_DEV, F_DEV), 1
    )
    one, zero = jnp.ones((), F32), jnp.zeros((), F32)
    earlier = jnp.dot(
        jnp.where(owned, one, zero).astype(BF16),
        jnp.where(before, one, zero).astype(BF16),
        preferred_element_type=F32,
    )
    rank = jnp.sum(jnp.where(owned, earlier, zero), axis=0, keepdims=True)
    place = owner.astype(F32) * float(per) + rank
    row_of = lax.broadcasted_iota(jnp.int32, (F_DEV, F_DEV), 0).astype(F32)
    sort_ref[...] = jnp.where(row_of == place, one, zero).astype(BF16)
    slot_f32 = (slot_row - owner * F_DEV).astype(F32)

    c = [jnp.broadcast_to(coupling_ref[pl.ds(h, 1), :], (BLOCKS, LANES)) for h in range(HALVES)]
    sublane = lax.broadcasted_iota(jnp.int32, (BLOCKS, LANES), 0)
    at_first = jnp.where((sublane == 0) & (wav == 0), one, zero)
    at_last = jnp.where((sublane == BLOCKS - 1) & (wav == n_wav - 1), one, zero)
    link_first = [2.0 * c[h] - c[h] * at_first for h in range(HALVES)]
    link_last = [2.0 * c[h] - c[h] * at_last for h in range(HALVES)]

    usable = []
    for chain in range(chains):
        e, h = chain // HALVES, chain % HALVES
        observed = (exp * e_dev + e) < counts_ref[pl.ds(h, 1), :]
        good = good_ref[pl.ds(e, 1), pl.ds(h * LANES, LANES)]
        usable.append(jnp.where(observed, good, 0) * ((1 << BITS) - 1))
    usable = [jnp.broadcast_to(u, (BLOCKS, LANES)) for u in usable]

    for copy in loads[: 2 * chains]:
        copy.wait()

    def spread(i):
        return pl.ds(i, BLOCKS, stride=step_count)

    def word_steps(k, _):
        kept_words = [
            bits[chain, pl.ds(k, BLOCKS, stride=words), :] & usable[chain]
            for chain in range(chains)
        ]

        def weigh(j, _):
            i = k * BITS + j
            first = jnp.where(i == 0, 1.0, 0.0)
            last = jnp.where(i == step_count - 1, 1.0, 0.0)
            for h in range(HALVES):
                both = 4.0 * c[h] - 2.0 * c[h] * (at_first * first + at_last * last)
                w_sum = band = None
                for e in range(e_dev):
                    chain = e * HALVES + h
                    iv = ivar[chain, spread(i), :]
                    bit = (kept_words[chain] >> j) & 1
                    w = jnp.where(bit == 1, iv, 0.0)
                    weight[i, chain] = w
                    part = w / (iv + both)
                    w_sum = w if w_sum is None else w_sum + w
                    band = part if band is None else band + part
                sums[0, h, spread(i), :] = w_sum
                sums[1, h, spread(i), :] = band * c[h]
            return 0

        return lax.fori_loop(0, BITS, weigh, 0)

    lax.fori_loop(0, words, word_steps, 0)

    pl.semaphore_wait(barrier, n_fib + 2)

    other_half = pl.ds(pl.multiple_of(partner * half, 8), half)
    my_half = pl.ds(pl.multiple_of(exp * half, 8), half)

    def half_copy(start, count, number):
        return pltpu.make_async_remote_copy(
            sums.at[pl.ds(start, count), :, other_half, :],
            theirs.at[pl.ds(start, count)],
            half_send.at[number],
            half_recv.at[number],
            **to(exp=partner),
        )

    half_a = half_copy(0, 2, 0)
    half_a.start()

    for copy in loads[2 * chains :]:
        copy.wait()

    c_e = [c[h][:e_dev] for h in range(HALVES)]

    def edge_row(ref, h, row):
        return jnp.concatenate(
            [ref[e * HALVES + h, pl.ds(row, 1), :] for e in range(e_dev)], axis=0
        )

    def edge_step(j, state):
        out = []
        for side in range(2):
            for h in range(HALVES):
                d, y = state[side * HALVES + h]
                row = waves - HALO + j if side == 0 else HALO - 1 - j
                iv, px = edge_row(ivar, h, row), edge_row(pix, h, row)
                m = c_e[h] / d
                out.append((iv + 2.0 * c_e[h] - c_e[h] * m, iv * px + m * y))
        return tuple(out)

    start = []
    for side in range(2):
        for h in range(HALVES):
            row = waves - HALO if side == 0 else HALO - 1
            iv, px = edge_row(ivar, h, row), edge_row(pix, h, row)
            start.append((iv + c_e[h], iv * px))
    ends = lax.fori_loop(1, HALO, edge_step, tuple(start))
    for side in range(2):
        for h in range(HALVES):
            for q in range(2):
                edge_out[side, q, pl.ds(h, e_dev, stride=HALVES), :] = ends[side * HALVES + h][q]

    def edge_copy(side):
        return pltpu.make_async_remote_copy(
            edge_out.at[side],
            edge_in.at[side],
            edge_send.at[side],
            edge_recv.at[side],
            **to(wav=wav_right if side == 0 else wav_left),
        )

    edges = [edge_copy(0), edge_copy(1)]
    for copy in edges:
        copy.start()

    def sorted_rows(number, extra):
        mine = [
            sums[number, h, my_half, :] + theirs[number, h, :, :] for h in range(HALVES)
        ]
        x = jnp.concatenate([jnp.concatenate(mine, axis=1), extra], axis=0)
        return exact_dot(sort_ref[...], x, ((1,), (1,)), True)

    def owner_copy(k, src, dst, s_sem, r_sem):
        p = fib_peer(k)
        return pltpu.make_async_remote_copy(
            src.at[pl.ds(pl.multiple_of(p * per, 8), per), :],
            dst.at[pl.ds(pl.multiple_of(fib * per, 8), per), :],
            s_sem.at[k],
            r_sem.at[k],
            **to(fib=p),
        )

    def send_all(src, dst, s_sem, r_sem):
        def one_peer(k, _):
            owner_copy(k, src, dst, s_sem, r_sem).start()
            return 0

        lax.fori_loop(1, n_fib, one_peer, 0)
        mine = pl.ds(pl.multiple_of(fib * per, 8), per)
        dst[mine, :] = src[mine, :]

    def wait_all(src, dst, s_sem, r_sem):
        def one_peer(k, _):
            owner_copy(k, src, dst, s_sem, r_sem).wait()
            return 0

        lax.fori_loop(1, n_fib, one_peer, 0)

    pad = ROWS - half
    blank = jnp.zeros((pad, F_DEV), F32)
    slot_rows = jnp.where(
        lax.broadcasted_iota(jnp.int32, (pad, F_DEV), 0) == SLOT_ROW - half,
        jnp.broadcast_to(slot_f32, (pad, F_DEV)),
        blank,
    )

    half_a.wait()
    send_a[:, pl.ds(0, ROWS)] = sorted_rows(0, slot_rows)
    send_a[:, pl.ds(ROWS, ROWS)] = sorted_rows(1, blank)
    send_all(send_a, got_a, a_send, a_recv)

    def eliminate(i, link, state):
        out = []
        for chain in range(chains):
            h = chain % HALVES
            m, y, s, g, hh = state[chain]
            iv = ivar[chain, spread(i), :]
            b = iv * pix[chain, spread(i), :]
            d = iv + link[h] - c[h] * m
            y = b + m * y
            s = m * s if s is not None else c[h]
            r = 1.0 / d
            m = c[h] * r
            q = s * r
            g = g + q * s
            hh = hh + q * y
            fac_m[i, chain] = m
            fac_y[i, chain] = r * y
            fac_q[i, chain] = q
            out.append((m, y, s, g, hh))
        return tuple(out)

    nothing = jnp.zeros((BLOCKS, LANES), F32)
    state = eliminate(0, link_first, tuple((nothing, nothing, None, nothing, nothing) for _ in range(chains)))
    link_inner = [2.0 * c[h] for h in range(HALVES)]
    last = step_count - 1
    state = lax.fori_loop(1, last, lambda i, st: eliminate(i, link_inner, st), state)

    for chain in range(chains):
        h = chain % HALVES
        m, y, s, g, hh = state[chain]
        iv = ivar[chain, spread(last), :]
        b = iv * pix[chain, spread(last), :]
        rows = pl.ds(chain * BLOCKS, BLOCKS)
        red[0, rows, :] = iv + link_last[h] - c[h] * m
        red[1, rows, :] = b + m * y
        red[2, rows, :] = g
        red[3, rows, :] = hh
        red[4, rows, :] = c[h] * fac_q[last - 1, chain]
        red[5, pl.ds(chain, 1), :] = coupling_ref[pl.ds(h, 1), :]

    for copy in edges:
        copy.wait()

    def across(k, b):
        return red[k, pl.ds(b, chains, stride=BLOCKS), :]

    d_l, y_l = edge_in[0, 0], edge_in[0, 1]
    d_r, y_r = edge_in[1, 0], edge_in[1, 1]
    c_all = red[5, pl.ds(0, chains), :]
    e_b = [across(4, b) for b in range(BLOCKS)]
    d_b, z_b = [], []
    right = c_all / d_r
    for b in range(BLOCKS):
        if b + 1 < BLOCKS:
            g_next, h_next = across(2, b + 1), across(3, b + 1)
        else:
            g_next = jnp.where(wav < n_wav - 1, c_all * right, 0.0)
            h_next = jnp.where(wav < n_wav - 1, y_r * right, 0.0)
        d_b.append(across(0, b) - g_next)
        z_b.append(across(1, b) + h_next)
    r_l = jnp.where(wav > 0, 1.0 / (d_l - across(2, 0)), 0.0)
    p_l = jnp.where(wav > 0, y_l + across(3, 0), 0.0)
    prev_e = e_b[0] * r_l
    d_b[0] = d_b[0] - e_b[0] * prev_e
    z_b[0] = z_b[0] + p_l * prev_e
    inv = []
    for b in range(BLOCKS):
        inv.append(1.0 / d_b[b])
        if b + 1 < BLOCKS:
            prev_e = e_b[b + 1] * inv[b]
            d_b[b + 1] = d_b[b + 1] - e_b[b + 1] * prev_e
            z_b[b + 1] = z_b[b + 1] + z_b[b] * prev_e
    x = None
    for b in reversed(range(BLOCKS)):
        x = inv[b] * (z_b[b] if x is None else z_b[b] + e_b[b + 1] * x)
        far[0, pl.ds(b, chains, stride=BLOCKS), :] = x
        if b + 1 < BLOCKS:
            far[1, pl.ds(b + 1, chains, stride=BLOCKS), :] = x
    far[1, pl.ds(0, chains, stride=BLOCKS), :] = r_l * (p_l + e_b[0] * x)

    def flux_at(i, xs):
        for h in range(HALVES):
            total = None
            for e in range(e_dev):
                chain = e * HALVES + h
                part = weight[i, chain] * xs[chain]
                total = part if total is None else total + part
            sums[2, h, spread(i), :] = total

    xs = [far[0, pl.ds(chain * BLOCKS, BLOCKS), :] for chain in range(chains)]
    lefts = [far[1, pl.ds(chain * BLOCKS, BLOCKS), :] for chain in range(chains)]
    flux_at(last, xs)

    def substitute(k, xs):
        i = last - 1 - k
        xs = tuple(
            fac_y[i, chain] + fac_q[i, chain] * lefts[chain] + fac_m[i, chain] * xs[chain]
            for chain in range(chains)
        )
        flux_at(i, xs)
        return xs

    lax.fori_loop(0, last, substitute, tuple(xs))

    half_b = half_copy(2, 1, 1)
    half_b.start()
    half_b.wait()
    send_b[...] = sorted_rows(2, blank)
    send_all(send_b, got_b, b_send, b_recv)
    wait_all(send_a, got_a, a_send, a_recv)
    wait_all(send_b, got_b, b_send, b_recv)


def finish_kernel(n_wav, a_ref, b_ref, flux_ref, ivar_ref, res_ref):
    wav, exp = lax.axis_index("wav"), lax.axis_index("exp")
    half = flux_ref.shape[0]
    slot = a_ref[:, pl.ds(SLOT_ROW, 1)]
    lane = lax.broadcasted_iota(jnp.int32, (F_DEV, F_DEV), 1).astype(F32)
    one, zero = jnp.ones((), F32), jnp.zeros((), F32)
    place = jnp.where(slot == lane, one, zero).astype(BF16)

    def placed(x):
        return exact_dot(place, x.T, ((1,), (0,)), False)[:half]

    weight_sum = placed(a_ref[:, pl.ds(0, ROWS)])
    band = placed(a_ref[:, pl.ds(ROWS, ROWS)])
    flux_sum = placed(b_ref[...])
    row = lax.broadcasted_iota(jnp.int32, (half, F_DEV), 0)
    first = (row == 0) & (wav == 0) & (exp == 0)
    last = (row == half - 1) & (wav == n_wav - 1) & (exp == 1)
    lower = jnp.where(first, 0.0, band)
    upper = jnp.where(last, 0.0, band)
    divisor = jnp.maximum(weight_sum, 1.0)
    flux_ref[...] = flux_sum / divisor
    ivar_ref[...] = weight_sum
    res_ref[0] = lower / divisor
    res_ref[1] = (weight_sum - lower - upper) / divisor
    res_ref[2] = upper / divisor


def per_device(n_fib, n_wav, pixels, pixel_ivar, clip_bits, coupling, counts, good_flags, owner_slot):
    e_dev, waves, _ = pixels.shape
    n_words = clip_bits.shape[1]
    chains = e_dev * HALVES
    steps = waves // BLOCKS
    half = waves // 2
    vmem = pl.BlockSpec(memory_space=pltpu.VMEM)
    hbm = pl.BlockSpec(memory_space=pl.ANY)
    dma = pltpu.SemaphoreType.DMA
    got_a, got_b = pl.pallas_call(
        functools.partial(exchange_kernel, n_fib, n_wav),
        out_shape=(
            jax.ShapeDtypeStruct((F_DEV, 2 * ROWS), F32),
            jax.ShapeDtypeStruct((F_DEV, ROWS), F32),
        ),
        in_specs=[hbm] * 3 + [vmem] * 4,
        out_specs=(vmem, vmem),
        scratch_shapes=[
            pltpu.VMEM((chains, waves, LANES), F32),
            pltpu.VMEM((chains, waves, LANES), F32),
            pltpu.VMEM((chains, n_words, LANES), jnp.int32),
            pltpu.VMEM((steps, chains, BLOCKS, LANES), F32),
            pltpu.VMEM((steps, chains, BLOCKS, LANES), F32),
            pltpu.VMEM((steps, chains, BLOCKS, LANES), F32),
            pltpu.VMEM((steps, chains, BLOCKS, LANES), F32),
            pltpu.VMEM((3, HALVES, waves, LANES), F32),
            pltpu.VMEM((3, HALVES, half, LANES), F32),
            pltpu.VMEM((F_DEV, 2 * ROWS), F32),
            pltpu.VMEM((F_DEV, ROWS), F32),
            pltpu.VMEM((F_DEV, F_DEV), BF16),
            pltpu.VMEM((2, 2, chains, LANES), F32),
            pltpu.VMEM((2, 2, chains, LANES), F32),
            pltpu.VMEM((6, chains * BLOCKS, LANES), F32),
            pltpu.VMEM((2, chains * BLOCKS, LANES), F32),
            dma((3, chains)),
            dma((2,)),
            dma((2,)),
            dma((2,)),
            dma((2,)),
            dma((n_fib,)),
            dma((n_fib,)),
            dma((n_fib,)),
            dma((n_fib,)),
        ],
        compiler_params=pltpu.CompilerParams(collective_id=0, has_side_effects=True),
        name="exchange",
    )(
        pixels,
        pixel_ivar,
        clip_bits,
        coupling.reshape(HALVES, LANES),
        counts.reshape(HALVES, LANES),
        good_flags,
        owner_slot.reshape(-1, LANES),
    )
    return pl.pallas_call(
        functools.partial(finish_kernel, n_wav),
        out_shape=(
            jax.ShapeDtypeStruct((half, F_DEV), F32),
            jax.ShapeDtypeStruct((half, F_DEV), F32),
            jax.ShapeDtypeStruct((3, half, F_DEV), F32),
        ),
        in_specs=[vmem, vmem],
        out_specs=(vmem, vmem, vmem),
        name="finish",
    )(got_a, got_b)


def solution(mesh):
    return jax.shard_map(
        functools.partial(per_device, mesh.shape["fib"], mesh.shape["wav"]),
        mesh=mesh,
        in_specs=(
            P("exp", "wav", "fib"),
            P("exp", "wav", "fib"),
            P("exp", "wav", "fib"),
            P("fib"),
            P("fib"),
            P("exp", "fib"),
            P(),
        ),
        out_specs=(
            P(("wav", "exp"), "fib"),
            P(("wav", "exp"), "fib"),
            P(None, ("wav", "exp"), "fib"),
        ),
        check_vma=False,
    )
```

```python
import functools

import jax
import jax.numpy as jnp
from jax import lax
from jax.experimental import pallas as pl
from jax.experimental.pallas import tpu as pltpu
from jax.sharding import PartitionSpec as P

HALO = 50
BLOCKS = 8
BITS = 15
LANES = 128
HALVES = 2
F_DEV = LANES * HALVES
ROWS = 256
SLOT_ROW = 240
RING = 8

F32 = jnp.float32
BF16 = jnp.bfloat16


def pieces(x):
    high = x.astype(BF16)
    rest = x - high.astype(F32)
    middle = rest.astype(BF16)
    low = (rest - middle.astype(F32)).astype(BF16)
    return high, middle, low


def exact_dot(one_hot, x, dims, one_hot_first):
    total = None
    for piece in pieces(x):
        pair = (one_hot, piece) if one_hot_first else (piece, one_hot)
        part = lax.dot_general(*pair, (dims, ((), ())), preferred_element_type=F32)
        total = part if total is None else total + part
    return total


def offsets(n_fib):
    n_z = RING if n_fib % RING == 0 else n_fib
    n_y = n_fib // n_z

    def hops(o):
        return min(o[0], n_y - o[0]) + min(o[1], n_z - o[1])

    others = [(dy, dz) for dy in range(n_y) for dz in range(n_z) if dy or dz]
    return n_y, n_z, sorted(others, key=lambda o: -hops(o))


def placed_rows(place, x, count):
    return exact_dot(place, x.T, ((1,), (0,)), False)[:count]


def exchange_kernel(
    n_fib,
    n_wav,
    pix_hbm,
    ivar_hbm,
    bits_hbm,
    coupling_ref,
    counts_ref,
    good_ref,
    slots_ref,
    place_ref,
    ivar_out,
    res_out,
    got_f,
    pix,
    ivar,
    bits,
    weight,
    fac_m,
    fac_y,
    fac_q,
    sums,
    theirs,
    send,
    got_w,
    got_t,
    sort_ref,
    edge_out,
    edge_in,
    red,
    far,
    load_sem,
    edge_send,
    edge_recv,
    half_send,
    half_recv,
    own_send,
    own_recv,
):
    fib, wav, exp = lax.axis_index("fib"), lax.axis_index("wav"), lax.axis_index("exp")
    e_dev = good_ref.shape[0]
    chains = e_dev * HALVES
    waves = ivar.shape[1]
    step_count = waves // BLOCKS
    words = bits.shape[1] // BLOCKS
    half = waves // 2
    per = F_DEV // n_fib

    def to(**where):
        return {"device_id": where, "device_id_type": pl.DeviceIdType.MESH}

    n_y, n_z, others = offsets(n_fib)
    fib_y, fib_z = fib // n_z, lax.rem(fib, n_z)

    def fib_peer(k):
        dy, dz = others[k]
        return lax.rem(fib_y + dy, n_y) * n_z + lax.rem(fib_z + dz, n_z)

    wav_right = lax.rem(wav + 1, n_wav)
    wav_left = lax.rem(wav + n_wav - 1, n_wav)
    partner = 1 - exp

    barrier = pltpu.get_barrier_semaphore()

    for k in range(n_fib - 1):
        pl.semaphore_signal(barrier, inc=1, **to(fib=fib_peer(k)))
    pl.semaphore_signal(barrier, inc=1, **to(exp=partner))
    pl.semaphore_signal(barrier, inc=1, **to(wav=wav_right))
    pl.semaphore_signal(barrier, inc=1, **to(wav=wav_left))

    loads = []

    def load(src, dst, rows, number):
        for chain in range(chains):
            e, h = chain // HALVES, chain % HALVES
            copy = pltpu.make_async_copy(
                src.at[e, :, pl.ds(h * LANES, LANES)], dst.at[chain], load_sem.at[number, chain]
            )
            copy.start()
            loads.append(copy)

    load(bits_hbm, bits, None, 0)
    load(ivar_hbm, ivar, None, 1)
    load(pix_hbm, pix, None, 2)

    slot_row = jnp.concatenate(
        [slots_ref[pl.ds(fib * HALVES + h, 1), :] for h in range(HALVES)], axis=1
    )
    owner = slot_row // F_DEV
    owned = owner == lax.broadcasted_iota(jnp.int32, (n_fib, F_DEV), 0)
    before = lax.broadcasted_iota(jnp.int32, (F_DEV, F_DEV), 0) < lax.broadcasted_iota(
        jnp.int32, (F_DEV, F_DEV), 1
    )
    one, zero = jnp.ones((), F32), jnp.zeros((), F32)
    earlier = jnp.dot(
        jnp.where(owned, one, zero).astype(BF16),
        jnp.where(before, one, zero).astype(BF16),
        preferred_element_type=F32,
    )
    rank = jnp.sum(jnp.where(owned, earlier, zero), axis=0, keepdims=True)
    place = owner.astype(F32) * float(per) + rank
    row_of = lax.broadcasted_iota(jnp.int32, (F_DEV, F_DEV), 0).astype(F32)
    sort_ref[...] = jnp.where(row_of == place, one, zero).astype(BF16)
    slot_f32 = (slot_row - owner * F_DEV).astype(F32)

    c = [jnp.broadcast_to(coupling_ref[pl.ds(h, 1), :], (BLOCKS, LANES)) for h in range(HALVES)]
    sublane = lax.broadcasted_iota(jnp.int32, (BLOCKS, LANES), 0)
    at_first = jnp.where((sublane == 0) & (wav == 0), one, zero)
    at_last = jnp.where((sublane == BLOCKS - 1) & (wav == n_wav - 1), one, zero)
    link_first = [2.0 * c[h] - c[h] * at_first for h in range(HALVES)]
    link_last = [2.0 * c[h] - c[h] * at_last for h in range(HALVES)]

    usable = []
    for chain in range(chains):
        e, h = chain // HALVES, chain % HALVES
        observed = (exp * e_dev + e) < counts_ref[pl.ds(h, 1), :]
        good = good_ref[pl.ds(e, 1), pl.ds(h * LANES, LANES)]
        usable.append(jnp.where(observed, good, 0) * ((1 << BITS) - 1))
    usable = [jnp.broadcast_to(u, (BLOCKS, LANES)) for u in usable]

    for copy in loads[: 2 * chains]:
        copy.wait()

    def spread(i):
        return pl.ds(i, BLOCKS, stride=step_count)

    def word_steps(k, _):
        kept_words = [
            bits[chain, pl.ds(k, BLOCKS, stride=words), :] & usable[chain]
            for chain in range(chains)
        ]

        def weigh(j, _):
            i = k * BITS + j
            for h in range(HALVES):
                w_sum = None
                for e in range(e_dev):
                    chain = e * HALVES + h
                    bit = (kept_words[chain] >> j) & 1
                    w = jnp.where(bit == 1, ivar[chain, spread(i), :], 0.0)
                    weight[i, chain] = w
                    w_sum = w if w_sum is None else w_sum + w
                sums[0, h, spread(i), :] = w_sum
            return 0

        return lax.fori_loop(0, BITS, weigh, 0)

    lax.fori_loop(0, words, word_steps, 0)

    pl.semaphore_wait(barrier, n_fib + 2)

    other_half = pl.ds(pl.multiple_of(partner * half, 8), half)
    my_half = pl.ds(pl.multiple_of(exp * half, 8), half)

    def half_copy(number):
        return pltpu.make_async_remote_copy(
            sums.at[number, :, other_half, :],
            theirs.at[number],
            half_send.at[number],
            half_recv.at[number],
            **to(exp=partner),
        )

    half_w = half_copy(0)
    half_w.start()

    def band_step(i, _):
        first = jnp.where(i == 0, 1.0, 0.0)
        last = jnp.where(i == step_count - 1, 1.0, 0.0)
        for h in range(HALVES):
            both = 4.0 * c[h] - 2.0 * c[h] * (at_first * first + at_last * last)
            band = None
            for e in range(e_dev):
                chain = e * HALVES + h
                part = weight[i, chain] / (ivar[chain, spread(i), :] + both)
                band = part if band is None else band + part
            sums[1, h, spread(i), :] = band * c[h]
        return 0

    lax.fori_loop(0, step_count, band_step, 0)
    half_t = half_copy(1)
    half_t.start()

    def sorted_rows(number, extra):
        mine = [
            sums[number, h, my_half, :] + theirs[number, h, :, :] for h in range(HALVES)
        ]
        x = jnp.concatenate([jnp.concatenate(mine, axis=1), extra], axis=0)
        return exact_dot(sort_ref[...], x, ((1,), (1,)), True)

    got = (got_w, got_t, got_f)
    mine = pl.ds(pl.multiple_of(fib * per, 8), per)

    def owner_copy(number, k):
        p = fib_peer(k)
        return pltpu.make_async_remote_copy(
            send.at[number, pl.ds(pl.multiple_of(p * per, 8), per), :],
            got[number].at[mine, :],
            own_send.at[number, k],
            own_recv.at[number, k],
            **to(fib=p),
        )

    def send_all(number, extra):
        send[number] = sorted_rows(number, extra)
        for k in range(n_fib - 1):
            owner_copy(number, k).start()
        got[number][mine, :] = send[number, mine, :]

    def wait_all(number):
        for k in range(n_fib - 1):
            owner_copy(number, k).wait()

    pad = ROWS - half
    blank = jnp.zeros((pad, F_DEV), F32)
    slot_rows = jnp.where(
        lax.broadcasted_iota(jnp.int32, (pad, F_DEV), 0) == SLOT_ROW - half,
        jnp.broadcast_to(slot_f32, (pad, F_DEV)),
        blank,
    )
    half_w.wait()
    send_all(0, slot_rows)

    for copy in loads[2 * chains :]:
        copy.wait()

    c_e = [c[h][:e_dev] for h in range(HALVES)]

    def edge_row(ref, h, row):
        return jnp.concatenate(
            [ref[e * HALVES + h, pl.ds(row, 1), :] for e in range(e_dev)], axis=0
        )

    def edge_step(j, state):
        out = []
        for side in range(2):
            for h in range(HALVES):
                d, y = state[side * HALVES + h]
                row = waves - HALO + j if side == 0 else HALO - 1 - j
                iv, px = edge_row(ivar, h, row), edge_row(pix, h, row)
                m = c_e[h] / d
                out.append((iv + 2.0 * c_e[h] - c_e[h] * m, iv * px + m * y))
        return tuple(out)

    start = []
    for side in range(2):
        for h in range(HALVES):
            row = waves - HALO if side == 0 else HALO - 1
            iv, px = edge_row(ivar, h, row), edge_row(pix, h, row)
            start.append((iv + c_e[h], iv * px))
    ends = lax.fori_loop(1, HALO, edge_step, tuple(start))
    for side in range(2):
        for h in range(HALVES):
            for q in range(2):
                edge_out[side, q, pl.ds(h, e_dev, stride=HALVES), :] = ends[side * HALVES + h][q]

    def edge_copy(side):
        return pltpu.make_async_remote_copy(
            edge_out.at[side],
            edge_in.at[side],
            edge_send.at[side],
            edge_recv.at[side],
            **to(wav=wav_right if side == 0 else wav_left),
        )

    edges = [edge_copy(0), edge_copy(1)]
    for copy in edges:
        copy.start()

    half_t.wait()
    send_all(1, blank)

    def eliminate(i, link, state):
        out = []
        for chain in range(chains):
            h = chain % HALVES
            m, y, s, g, hh = state[chain]
            iv = ivar[chain, spread(i), :]
            b = iv * pix[chain, spread(i), :]
            d = iv + link[h] - c[h] * m
            y = b + m * y
            s = m * s if s is not None else c[h]
            r = 1.0 / d
            m = c[h] * r
            q = s * r
            g = g + q * s
            hh = hh + q * y
            fac_m[i, chain] = m
            fac_y[i, chain] = r * y
            fac_q[i, chain] = q
            out.append((m, y, s, g, hh))
        return tuple(out)

    nothing = jnp.zeros((BLOCKS, LANES), F32)
    state = eliminate(0, link_first, tuple((nothing, nothing, None, nothing, nothing) for _ in range(chains)))
    link_inner = [2.0 * c[h] for h in range(HALVES)]
    last = step_count - 1
    state = lax.fori_loop(1, last, lambda i, st: eliminate(i, link_inner, st), state)

    for chain in range(chains):
        h = chain % HALVES
        m, y, s, g, hh = state[chain]
        iv = ivar[chain, spread(last), :]
        b = iv * pix[chain, spread(last), :]
        rows = pl.ds(chain * BLOCKS, BLOCKS)
        red[0, rows, :] = iv + link_last[h] - c[h] * m
        red[1, rows, :] = b + m * y
        red[2, rows, :] = g
        red[3, rows, :] = hh
        red[4, rows, :] = c[h] * fac_q[last - 1, chain]
        red[5, pl.ds(chain, 1), :] = coupling_ref[pl.ds(h, 1), :]

    for copy in edges:
        copy.wait()

    def across(k, b):
        return red[k, pl.ds(b, chains, stride=BLOCKS), :]

    d_l, y_l = edge_in[0, 0], edge_in[0, 1]
    d_r, y_r = edge_in[1, 0], edge_in[1, 1]
    c_all = red[5, pl.ds(0, chains), :]
    e_b = [across(4, b) for b in range(BLOCKS)]
    d_b, z_b = [], []
    right = c_all / d_r
    for b in range(BLOCKS):
        if b + 1 < BLOCKS:
            g_next, h_next = across(2, b + 1), across(3, b + 1)
        else:
            g_next = jnp.where(wav < n_wav - 1, c_all * right, 0.0)
            h_next = jnp.where(wav < n_wav - 1, y_r * right, 0.0)
        d_b.append(across(0, b) - g_next)
        z_b.append(across(1, b) + h_next)
    r_l = jnp.where(wav > 0, 1.0 / (d_l - across(2, 0)), 0.0)
    p_l = jnp.where(wav > 0, y_l + across(3, 0), 0.0)
    prev_e = e_b[0] * r_l
    d_b[0] = d_b[0] - e_b[0] * prev_e
    z_b[0] = z_b[0] + p_l * prev_e
    inv = []
    for b in range(BLOCKS):
        inv.append(1.0 / d_b[b])
        if b + 1 < BLOCKS:
            prev_e = e_b[b + 1] * inv[b]
            d_b[b + 1] = d_b[b + 1] - e_b[b + 1] * prev_e
            z_b[b + 1] = z_b[b + 1] + z_b[b] * prev_e
    x = None
    for b in reversed(range(BLOCKS)):
        x = inv[b] * (z_b[b] if x is None else z_b[b] + e_b[b + 1] * x)
        far[0, pl.ds(b, chains, stride=BLOCKS), :] = x
        if b + 1 < BLOCKS:
            far[1, pl.ds(b + 1, chains, stride=BLOCKS), :] = x
    far[1, pl.ds(0, chains, stride=BLOCKS), :] = r_l * (p_l + e_b[0] * x)

    def flux_at(i, xs):
        for h in range(HALVES):
            total = None
            for e in range(e_dev):
                chain = e * HALVES + h
                part = weight[i, chain] * xs[chain]
                total = part if total is None else total + part
            sums[2, h, spread(i), :] = total

    xs = [far[0, pl.ds(chain * BLOCKS, BLOCKS), :] for chain in range(chains)]
    lefts = [far[1, pl.ds(chain * BLOCKS, BLOCKS), :] for chain in range(chains)]
    flux_at(last, xs)

    def substitute(k, xs):
        i = last - 1 - k
        xs = tuple(
            fac_y[i, chain] + fac_q[i, chain] * lefts[chain] + fac_m[i, chain] * xs[chain]
            for chain in range(chains)
        )
        flux_at(i, xs)
        return xs

    lax.fori_loop(0, last, substitute, tuple(xs))

    half_f = half_copy(2)
    half_f.start()
    half_f.wait()
    send_all(2, blank)

    wait_all(0)
    slot = got_w[:, pl.ds(SLOT_ROW, 1)]
    lane = lax.broadcasted_iota(jnp.int32, (F_DEV, F_DEV), 1).astype(F32)
    place_ref[...] = jnp.where(slot == lane, one, zero).astype(BF16)
    place = place_ref[...]
    ivar_out[...] = placed_rows(place, got_w[...], half)
    wait_all(1)
    band = placed_rows(place, got_t[...], half)
    weight_sum = ivar_out[...]
    row = lax.broadcasted_iota(jnp.int32, (half, F_DEV), 0)
    lower = jnp.where((row == 0) & (wav == 0) & (exp == 0), 0.0, band)
    upper = jnp.where((row == half - 1) & (wav == n_wav - 1) & (exp == 1), 0.0, band)
    divisor = jnp.maximum(weight_sum, 1.0)
    res_out[0] = lower / divisor
    res_out[1] = (weight_sum - lower - upper) / divisor
    res_out[2] = upper / divisor
    wait_all(2)


def finish_kernel(place_ref, ivar_ref, res_ref, got_ref, flux_hbm, ivar_hbm, res_hbm, flux, sems):
    half = ivar_ref.shape[0]
    copies = [
        pltpu.make_async_copy(ivar_ref, ivar_hbm, sems.at[0]),
        pltpu.make_async_copy(res_ref, res_hbm, sems.at[1]),
        pltpu.make_async_copy(flux, flux_hbm, sems.at[2]),
    ]
    copies[0].start()
    copies[1].start()
    flux[...] = placed_rows(place_ref[...], got_ref[...], half) / jnp.maximum(ivar_ref[...], 1.0)
    copies[2].start()
    for copy in copies:
        copy.wait()


def per_device(n_fib, n_wav, pixels, pixel_ivar, clip_bits, coupling, counts, good_flags, owner_slot):
    e_dev, waves, _ = pixels.shape
    n_words = clip_bits.shape[1]
    chains = e_dev * HALVES
    steps = waves // BLOCKS
    half = waves // 2
    vmem = pl.BlockSpec(memory_space=pltpu.VMEM)
    hbm = pl.BlockSpec(memory_space=pltpu.HBM)
    dma = pltpu.SemaphoreType.DMA
    limit = 24 * 2**20
    parts = pl.pallas_call(
        functools.partial(exchange_kernel, n_fib, n_wav),
        out_shape=(
            jax.ShapeDtypeStruct((F_DEV, F_DEV), BF16),
            jax.ShapeDtypeStruct((half, F_DEV), F32),
            jax.ShapeDtypeStruct((3, half, F_DEV), F32),
            jax.ShapeDtypeStruct((F_DEV, ROWS), F32),
        ),
        in_specs=[hbm] * 3 + [vmem] * 4,
        out_specs=(vmem,) * 4,
        scratch_shapes=[
            pltpu.VMEM((chains, waves, LANES), F32),
            pltpu.VMEM((chains, waves, LANES), F32),
            pltpu.VMEM((chains, n_words, LANES), jnp.int32),
            pltpu.VMEM((steps, chains, BLOCKS, LANES), F32),
            pltpu.VMEM((steps, chains, BLOCKS, LANES), F32),
            pltpu.VMEM((steps, chains, BLOCKS, LANES), F32),
            pltpu.VMEM((steps, chains, BLOCKS, LANES), F32),
            pltpu.VMEM((3, HALVES, waves, LANES), F32),
            pltpu.VMEM((3, HALVES, half, LANES), F32),
            pltpu.VMEM((3, F_DEV, ROWS), F32),
            pltpu.VMEM((F_DEV, ROWS), F32),
            pltpu.VMEM((F_DEV, ROWS), F32),
            pltpu.VMEM((F_DEV, F_DEV), BF16),
            pltpu.VMEM((2, 2, chains, LANES), F32),
            pltpu.VMEM((2, 2, chains, LANES), F32),
            pltpu.VMEM((6, chains * BLOCKS, LANES), F32),
            pltpu.VMEM((2, chains * BLOCKS, LANES), F32),
            dma((3, chains)),
            dma((2,)),
            dma((2,)),
            dma((3,)),
            dma((3,)),
            dma((3, n_fib - 1)),
            dma((3, n_fib - 1)),
        ],
        compiler_params=pltpu.CompilerParams(
            collective_id=0, has_side_effects=True, vmem_limit_bytes=limit
        ),
        name="exchange",
    )(
        *(
            pltpu.with_memory_space_constraint(x, pltpu.HBM)
            for x in (
                pixels,
                pixel_ivar,
                clip_bits,
                coupling.reshape(HALVES, LANES),
                counts.reshape(HALVES, LANES),
                good_flags,
                owner_slot.reshape(-1, LANES),
            )
        )
    )
    return pl.pallas_call(
        finish_kernel,
        out_shape=(
            jax.ShapeDtypeStruct((half, F_DEV), F32),
            jax.ShapeDtypeStruct((half, F_DEV), F32),
            jax.ShapeDtypeStruct((3, half, F_DEV), F32),
        ),
        in_specs=[vmem] * 4,
        out_specs=(hbm,) * 3,
        scratch_shapes=[pltpu.VMEM((half, F_DEV), F32), dma((3,))],
        compiler_params=pltpu.CompilerParams(vmem_limit_bytes=8 * 2**20),
        name="finish",
    )(*parts)


def solution(mesh):
    return jax.shard_map(
        functools.partial(per_device, mesh.shape["fib"], mesh.shape["wav"]),
        mesh=mesh,
        in_specs=(
            P("exp", "wav", "fib"),
            P("exp", "wav", "fib"),
            P("exp", "wav", "fib"),
            P("fib"),
            P("fib"),
            P("exp", "fib"),
            P(),
        ),
        out_specs=(
            P(("wav", "exp"), "fib"),
            P(("wav", "exp"), "fib"),
            P(None, ("wav", "exp"), "fib"),
        ),
        check_vma=False,
    )
```

```python
import functools

import jax
import jax.numpy as jnp
from jax import lax
from jax.experimental import pallas as pl
from jax.experimental.pallas import tpu as pltpu
from jax.sharding import PartitionSpec as P

HALO = 50
BLOCKS = 8
BITS = 15
LANES = 128
HALVES = 2
F_DEV = LANES * HALVES
TILES = 2
ROWS = LANES * TILES
SLOT_ROW = 240
RING = 8

F32 = jnp.float32
BF16 = jnp.bfloat16


def pieces(x):
    high = x.astype(BF16)
    rest = x - high.astype(F32)
    middle = rest.astype(BF16)
    low = (rest - middle.astype(F32)).astype(BF16)
    return high, middle, low


def exact_dot(one_hot, x, dims, one_hot_first):
    total = None
    for piece in pieces(x):
        pair = (one_hot, piece) if one_hot_first else (piece, one_hot)
        part = lax.dot_general(*pair, (dims, ((), ())), preferred_element_type=F32)
        total = part if total is None else total + part
    return total


def offsets(n_fib):
    n_z = RING if n_fib % RING == 0 else n_fib
    n_y = n_fib // n_z

    def hops(o):
        return min(o[0], n_y - o[0]) + min(o[1], n_z - o[1])

    others = [(dy, dz) for dy in range(n_y) for dz in range(n_z) if dy or dz]
    return n_y, n_z, sorted(others, key=lambda o: -hops(o))


def placed_rows(place, got_ref, count):
    x = jnp.concatenate([got_ref[tile].T for tile in range(TILES)], axis=0)
    return exact_dot(place, x, ((1,), (0,)), False)[:count]


def exchange_kernel(
    n_fib,
    n_wav,
    pix_hbm,
    ivar_hbm,
    bits_hbm,
    coupling_hbm,
    counts_hbm,
    good_hbm,
    slots_hbm,
    place_ref,
    ivar_out,
    res_out,
    got_f,
    coupling_ref,
    counts_ref,
    good_ref,
    slots_ref,
    pix,
    ivar,
    bits,
    weight,
    fac_m,
    fac_y,
    fac_q,
    sums,
    give,
    take,
    send,
    got_w,
    got_t,
    sort_ref,
    edge_out,
    edge_in,
    red,
    far,
    small_sem,
    load_sem,
    edge_send,
    edge_recv,
    half_send,
    half_recv,
    own_send,
    own_recv,
):
    fib, wav, exp = lax.axis_index("fib"), lax.axis_index("wav"), lax.axis_index("exp")
    e_dev = good_ref.shape[0]
    chains = e_dev * HALVES
    waves = ivar.shape[1]
    step_count = waves // BLOCKS
    words = bits.shape[1] // BLOCKS
    half = waves // 2
    per = F_DEV // n_fib

    def to(**where):
        return {"device_id": where, "device_id_type": pl.DeviceIdType.MESH}

    n_y, n_z, others = offsets(n_fib)
    fib_y, fib_z = fib // n_z, lax.rem(fib, n_z)

    def fib_peer(k):
        dy, dz = others[k]
        return lax.rem(fib_y + dy, n_y) * n_z + lax.rem(fib_z + dz, n_z)

    def fib_from(k):
        dy, dz = others[k]
        return lax.rem(fib_y + n_y - dy, n_y) * n_z + lax.rem(fib_z + n_z - dz, n_z)

    wav_right = lax.rem(wav + 1, n_wav)
    wav_left = lax.rem(wav + n_wav - 1, n_wav)
    partner = 1 - exp

    barrier = pltpu.get_barrier_semaphore()

    for k in range(n_fib - 1):
        pl.semaphore_signal(barrier, inc=1, **to(fib=fib_peer(k)))
    pl.semaphore_signal(barrier, inc=1, **to(exp=partner))
    pl.semaphore_signal(barrier, inc=1, **to(wav=wav_right))
    pl.semaphore_signal(barrier, inc=1, **to(wav=wav_left))

    small = [
        pltpu.make_async_copy(src, dst, small_sem.at[number])
        for number, (src, dst) in enumerate(
            (
                (slots_hbm, slots_ref),
                (coupling_hbm, coupling_ref),
                (counts_hbm, counts_ref),
                (good_hbm, good_ref),
            )
        )
    ]
    for copy in small:
        copy.start()
    loads = []

    def load(src, dst, rows, number):
        for chain in range(chains):
            e, h = chain // HALVES, chain % HALVES
            copy = pltpu.make_async_copy(
                src.at[e, :, pl.ds(h * LANES, LANES)], dst.at[chain], load_sem.at[number, chain]
            )
            copy.start()
            loads.append(copy)

    load(bits_hbm, bits, None, 0)
    load(ivar_hbm, ivar, None, 1)
    load(pix_hbm, pix, None, 2)

    for copy in small:
        copy.wait()

    slot_row = jnp.concatenate(
        [slots_ref[pl.ds(fib * HALVES + h, 1), :] for h in range(HALVES)], axis=1
    )
    owner = slot_row // F_DEV
    owned = owner == lax.broadcasted_iota(jnp.int32, (n_fib, F_DEV), 0)
    before = lax.broadcasted_iota(jnp.int32, (F_DEV, F_DEV), 0) < lax.broadcasted_iota(
        jnp.int32, (F_DEV, F_DEV), 1
    )
    one, zero = jnp.ones((), F32), jnp.zeros((), F32)
    earlier = jnp.dot(
        jnp.where(owned, one, zero).astype(BF16),
        jnp.where(before, one, zero).astype(BF16),
        preferred_element_type=F32,
    )
    rank = jnp.sum(jnp.where(owned, earlier, zero), axis=0, keepdims=True)
    place = owner.astype(F32) * float(per) + rank
    row_of = lax.broadcasted_iota(jnp.int32, (F_DEV, F_DEV), 0).astype(F32)
    sort_ref[...] = jnp.where(row_of == place, one, zero).astype(BF16)
    slot_f32 = (slot_row - owner * F_DEV).astype(F32)

    c = [jnp.broadcast_to(coupling_ref[pl.ds(h, 1), :], (BLOCKS, LANES)) for h in range(HALVES)]
    sublane = lax.broadcasted_iota(jnp.int32, (BLOCKS, LANES), 0)
    at_first = jnp.where((sublane == 0) & (wav == 0), one, zero)
    at_last = jnp.where((sublane == BLOCKS - 1) & (wav == n_wav - 1), one, zero)
    link_first = [2.0 * c[h] - c[h] * at_first for h in range(HALVES)]
    link_last = [2.0 * c[h] - c[h] * at_last for h in range(HALVES)]

    usable = []
    for chain in range(chains):
        e, h = chain // HALVES, chain % HALVES
        observed = (exp * e_dev + e) < counts_ref[pl.ds(h, 1), :]
        good = good_ref[pl.ds(e, 1), pl.ds(h * LANES, LANES)]
        usable.append(jnp.where(observed, good, 0) * ((1 << BITS) - 1))
    usable = [jnp.broadcast_to(u, (BLOCKS, LANES)) for u in usable]

    for copy in loads[: 2 * chains]:
        copy.wait()

    def spread(i):
        return pl.ds(i, BLOCKS, stride=step_count)

    def word_steps(k, _):
        kept_words = [
            bits[chain, pl.ds(k, BLOCKS, stride=words), :] & usable[chain]
            for chain in range(chains)
        ]

        def weigh(j, _):
            i = k * BITS + j
            for h in range(HALVES):
                w_sum = None
                for e in range(e_dev):
                    chain = e * HALVES + h
                    bit = (kept_words[chain] >> j) & 1
                    w = jnp.where(bit == 1, ivar[chain, spread(i), :], 0.0)
                    weight[i, chain] = w
                    w_sum = w if w_sum is None else w_sum + w
                sums[0, h, spread(i), :] = w_sum
            return 0

        return lax.fori_loop(0, BITS, weigh, 0)

    lax.fori_loop(0, words, word_steps, 0)

    pad = ROWS - half
    blank = jnp.zeros((pad, F_DEV), F32)
    slot_rows = jnp.where(
        lax.broadcasted_iota(jnp.int32, (pad, F_DEV), 0) == SLOT_ROW - half,
        jnp.broadcast_to(slot_f32, (pad, F_DEV)),
        blank,
    )
    my_half = pl.ds(pl.multiple_of(exp * half, 8), half)
    other_half = pl.ds(pl.multiple_of(partner * half, 8), half)

    def sort(number, rows, extra, dst):
        x = jnp.concatenate([sums[number, h, rows, :] for h in range(HALVES)], axis=1)
        x = jnp.concatenate([x, extra], axis=0)
        x = exact_dot(sort_ref[...], x, ((1,), (1,)), True)
        for tile in range(TILES):
            dst[number, tile] = x[:, tile * LANES : (tile + 1) * LANES]

    def give_copy(number, tile):
        return pltpu.make_async_remote_copy(
            give.at[number, tile],
            take.at[number, tile],
            half_send.at[number, tile],
            half_recv.at[number, tile],
            **to(exp=partner),
        )

    def give_all(number):
        for tile in range(TILES):
            give_copy(number, tile).start()
        sort(number, my_half, slot_rows if number == 0 else blank, send)

    got = (got_w, got_t, got_f)
    mine = pl.ds(pl.multiple_of(fib * per, 8), per)

    def owner_copy(number, k, source):
        p = pl.ds(pl.multiple_of(fib_peer(k) * per, 8), per)
        q = pl.ds(pl.multiple_of(source * per, 8), per)
        return pltpu.make_async_remote_copy(
            send.at[number, :, p, :],
            got[number].at[:, q, :],
            own_send.at[number, k],
            own_recv.at[number, k],
            **to(fib=fib_peer(k)),
        )

    def send_all(number):
        for tile in range(TILES):
            give_copy(number, tile).wait()
            send[number, tile] = send[number, tile] + take[number, tile]
            got[number][tile, mine, :] = send[number, tile, mine, :]
        for k in range(n_fib - 1):
            owner_copy(number, k, fib).start()

    def wait_all(number):
        for k in range(n_fib - 1):
            owner_copy(number, k, fib_from(k)).wait()

    sort(0, other_half, blank, give)
    pl.semaphore_wait(barrier, n_fib + 2)
    give_all(0)

    def band_step(i, _):
        first = jnp.where(i == 0, 1.0, 0.0)
        last = jnp.where(i == step_count - 1, 1.0, 0.0)
        for h in range(HALVES):
            both = 4.0 * c[h] - 2.0 * c[h] * (at_first * first + at_last * last)
            band = None
            for e in range(e_dev):
                chain = e * HALVES + h
                part = weight[i, chain] / (ivar[chain, spread(i), :] + both)
                band = part if band is None else band + part
            sums[1, h, spread(i), :] = band * c[h]
        return 0

    lax.fori_loop(0, step_count, band_step, 0)
    send_all(0)
    sort(1, other_half, blank, give)
    give_all(1)

    for copy in loads[2 * chains :]:
        copy.wait()

    c_e = [c[h][:e_dev] for h in range(HALVES)]

    def edge_row(ref, h, row):
        return jnp.concatenate(
            [ref[e * HALVES + h, pl.ds(row, 1), :] for e in range(e_dev)], axis=0
        )

    def edge_step(j, state):
        out = []
        for side in range(2):
            for h in range(HALVES):
                d, y = state[side * HALVES + h]
                row = waves - HALO + j if side == 0 else HALO - 1 - j
                iv, px = edge_row(ivar, h, row), edge_row(pix, h, row)
                m = c_e[h] / d
                out.append((iv + 2.0 * c_e[h] - c_e[h] * m, iv * px + m * y))
        return tuple(out)

    start = []
    for side in range(2):
        for h in range(HALVES):
            row = waves - HALO if side == 0 else HALO - 1
            iv, px = edge_row(ivar, h, row), edge_row(pix, h, row)
            start.append((iv + c_e[h], iv * px))
    ends = lax.fori_loop(1, HALO, edge_step, tuple(start))
    for side in range(2):
        for h in range(HALVES):
            for q in range(2):
                edge_out[side, q, pl.ds(h, e_dev, stride=HALVES), :] = ends[side * HALVES + h][q]

    def edge_copy(side):
        return pltpu.make_async_remote_copy(
            edge_out.at[side],
            edge_in.at[side],
            edge_send.at[side],
            edge_recv.at[side],
            **to(wav=wav_right if side == 0 else wav_left),
        )

    edges = [edge_copy(0), edge_copy(1)]
    for copy in edges:
        copy.start()
    send_all(1)

    def eliminate(i, link, state):
        out = []
        for chain in range(chains):
            h = chain % HALVES
            m, y, s, g, hh = state[chain]
            iv = ivar[chain, spread(i), :]
            b = iv * pix[chain, spread(i), :]
            d = iv + link[h] - c[h] * m
            y = b + m * y
            s = m * s if s is not None else c[h]
            r = 1.0 / d
            m = c[h] * r
            q = s * r
            g = g + q * s
            hh = hh + q * y
            fac_m[i, chain] = m
            fac_y[i, chain] = r * y
            fac_q[i, chain] = q
            out.append((m, y, s, g, hh))
        return tuple(out)

    nothing = jnp.zeros((BLOCKS, LANES), F32)
    state = eliminate(0, link_first, tuple((nothing, nothing, None, nothing, nothing) for _ in range(chains)))
    link_inner = [2.0 * c[h] for h in range(HALVES)]
    last = step_count - 1
    state = lax.fori_loop(1, last, lambda i, st: eliminate(i, link_inner, st), state)

    for chain in range(chains):
        h = chain % HALVES
        m, y, s, g, hh = state[chain]
        iv = ivar[chain, spread(last), :]
        b = iv * pix[chain, spread(last), :]
        rows = pl.ds(chain * BLOCKS, BLOCKS)
        red[0, rows, :] = iv + link_last[h] - c[h] * m
        red[1, rows, :] = b + m * y
        red[2, rows, :] = g
        red[3, rows, :] = hh
        red[4, rows, :] = c[h] * fac_q[last - 1, chain]
        red[5, pl.ds(chain, 1), :] = coupling_ref[pl.ds(h, 1), :]

    for copy in edges:
        copy.wait()

    def across(k, b):
        return red[k, pl.ds(b, chains, stride=BLOCKS), :]

    d_l, y_l = edge_in[0, 0], edge_in[0, 1]
    d_r, y_r = edge_in[1, 0], edge_in[1, 1]
    c_all = red[5, pl.ds(0, chains), :]
    e_b = [across(4, b) for b in range(BLOCKS)]
    d_b, z_b = [], []
    right = c_all / d_r
    for b in range(BLOCKS):
        if b + 1 < BLOCKS:
            g_next, h_next = across(2, b + 1), across(3, b + 1)
        else:
            g_next = jnp.where(wav < n_wav - 1, c_all * right, 0.0)
            h_next = jnp.where(wav < n_wav - 1, y_r * right, 0.0)
        d_b.append(across(0, b) - g_next)
        z_b.append(across(1, b) + h_next)
    r_l = jnp.where(wav > 0, 1.0 / (d_l - across(2, 0)), 0.0)
    p_l = jnp.where(wav > 0, y_l + across(3, 0), 0.0)
    prev_e = e_b[0] * r_l
    d_b[0] = d_b[0] - e_b[0] * prev_e
    z_b[0] = z_b[0] + p_l * prev_e
    inv = []
    for b in range(BLOCKS):
        inv.append(1.0 / d_b[b])
        if b + 1 < BLOCKS:
            prev_e = e_b[b + 1] * inv[b]
            d_b[b + 1] = d_b[b + 1] - e_b[b + 1] * prev_e
            z_b[b + 1] = z_b[b + 1] + z_b[b] * prev_e
    x = None
    for b in reversed(range(BLOCKS)):
        x = inv[b] * (z_b[b] if x is None else z_b[b] + e_b[b + 1] * x)
        far[0, pl.ds(b, chains, stride=BLOCKS), :] = x
        if b + 1 < BLOCKS:
            far[1, pl.ds(b + 1, chains, stride=BLOCKS), :] = x
    far[1, pl.ds(0, chains, stride=BLOCKS), :] = r_l * (p_l + e_b[0] * x)

    def flux_at(i, xs):
        for h in range(HALVES):
            total = None
            for e in range(e_dev):
                chain = e * HALVES + h
                part = weight[i, chain] * xs[chain]
                total = part if total is None else total + part
            sums[2, h, spread(i), :] = total

    xs = [far[0, pl.ds(chain * BLOCKS, BLOCKS), :] for chain in range(chains)]
    lefts = [far[1, pl.ds(chain * BLOCKS, BLOCKS), :] for chain in range(chains)]
    flux_at(last, xs)

    def substitute(k, xs):
        i = last - 1 - k
        xs = tuple(
            fac_y[i, chain] + fac_q[i, chain] * lefts[chain] + fac_m[i, chain] * xs[chain]
            for chain in range(chains)
        )
        flux_at(i, xs)
        return xs

    lax.fori_loop(0, last, substitute, tuple(xs))

    sort(2, other_half, blank, give)
    give_all(2)
    send_all(2)

    wait_all(0)
    slot = got_w[SLOT_ROW // LANES, :, pl.ds(SLOT_ROW % LANES, 1)]
    lane = lax.broadcasted_iota(jnp.int32, (F_DEV, F_DEV), 1).astype(F32)
    place_ref[...] = jnp.where(slot == lane, one, zero).astype(BF16)
    place = place_ref[...]
    ivar_out[...] = placed_rows(place, got_w, half)
    wait_all(1)
    band = placed_rows(place, got_t, half)
    weight_sum = ivar_out[...]
    row = lax.broadcasted_iota(jnp.int32, (half, F_DEV), 0)
    lower = jnp.where((row == 0) & (wav == 0) & (exp == 0), 0.0, band)
    upper = jnp.where((row == half - 1) & (wav == n_wav - 1) & (exp == 1), 0.0, band)
    divisor = jnp.maximum(weight_sum, 1.0)
    res_out[0] = lower / divisor
    res_out[1] = (weight_sum - lower - upper) / divisor
    res_out[2] = upper / divisor
    wait_all(2)


def finish_kernel(place_ref, ivar_ref, res_ref, got_ref, flux_hbm, ivar_hbm, res_hbm, flux, sems):
    half = ivar_ref.shape[0]
    copies = [
        pltpu.make_async_copy(ivar_ref, ivar_hbm, sems.at[0]),
        pltpu.make_async_copy(res_ref, res_hbm, sems.at[1]),
        pltpu.make_async_copy(flux, flux_hbm, sems.at[2]),
    ]
    copies[0].start()
    copies[1].start()
    flux[...] = placed_rows(place_ref[...], got_ref, half) / jnp.maximum(ivar_ref[...], 1.0)
    copies[2].start()
    for copy in copies:
        copy.wait()


def per_device(n_fib, n_wav, pixels, pixel_ivar, clip_bits, coupling, counts, good_flags, owner_slot):
    e_dev, waves, _ = pixels.shape
    n_words = clip_bits.shape[1]
    chains = e_dev * HALVES
    steps = waves // BLOCKS
    half = waves // 2
    vmem = pl.BlockSpec(memory_space=pltpu.VMEM)
    hbm = pl.BlockSpec(memory_space=pltpu.HBM)
    dma = pltpu.SemaphoreType.DMA
    limit = 24 * 2**20
    parts = pl.pallas_call(
        functools.partial(exchange_kernel, n_fib, n_wav),
        out_shape=(
            jax.ShapeDtypeStruct((F_DEV, F_DEV), BF16),
            jax.ShapeDtypeStruct((half, F_DEV), F32),
            jax.ShapeDtypeStruct((3, half, F_DEV), F32),
            jax.ShapeDtypeStruct((TILES, F_DEV, LANES), F32),
        ),
        in_specs=[hbm] * 7,
        out_specs=(vmem,) * 4,
        scratch_shapes=[
            pltpu.VMEM((HALVES, LANES), F32),
            pltpu.VMEM((HALVES, LANES), jnp.int32),
            pltpu.VMEM(good_flags.shape, jnp.int32),
            pltpu.VMEM((owner_slot.shape[0] // LANES, LANES), jnp.int32),
            pltpu.VMEM((chains, waves, LANES), F32),
            pltpu.VMEM((chains, waves, LANES), F32),
            pltpu.VMEM((chains, n_words, LANES), jnp.int32),
            pltpu.VMEM((steps, chains, BLOCKS, LANES), F32),
            pltpu.VMEM((steps, chains, BLOCKS, LANES), F32),
            pltpu.VMEM((steps, chains, BLOCKS, LANES), F32),
            pltpu.VMEM((steps, chains, BLOCKS, LANES), F32),
            pltpu.VMEM((3, HALVES, waves, LANES), F32),
            pltpu.VMEM((3, TILES, F_DEV, LANES), F32),
            pltpu.VMEM((3, TILES, F_DEV, LANES), F32),
            pltpu.VMEM((3, TILES, F_DEV, LANES), F32),
            pltpu.VMEM((TILES, F_DEV, LANES), F32),
            pltpu.VMEM((TILES, F_DEV, LANES), F32),
            pltpu.VMEM((F_DEV, F_DEV), BF16),
            pltpu.VMEM((2, 2, chains, LANES), F32),
            pltpu.VMEM((2, 2, chains, LANES), F32),
            pltpu.VMEM((6, chains * BLOCKS, LANES), F32),
            pltpu.VMEM((2, chains * BLOCKS, LANES), F32),
            dma((4,)),
            dma((3, chains)),
            dma((2,)),
            dma((2,)),
            dma((3, TILES)),
            dma((3, TILES)),
            dma((3, n_fib - 1)),
            dma((3, n_fib - 1)),
        ],
        compiler_params=pltpu.CompilerParams(
            collective_id=0, has_side_effects=True, vmem_limit_bytes=limit
        ),
        name="exchange",
    )(
        *(
            pltpu.with_memory_space_constraint(x, pltpu.HBM)
            for x in (
                pixels,
                pixel_ivar,
                clip_bits,
                coupling.reshape(HALVES, LANES),
                counts.reshape(HALVES, LANES),
                good_flags,
                owner_slot.reshape(-1, LANES),
            )
        )
    )
    return pl.pallas_call(
        finish_kernel,
        out_shape=(
            jax.ShapeDtypeStruct((half, F_DEV), F32),
            jax.ShapeDtypeStruct((half, F_DEV), F32),
            jax.ShapeDtypeStruct((3, half, F_DEV), F32),
        ),
        in_specs=[vmem] * 4,
        out_specs=(hbm,) * 3,
        scratch_shapes=[pltpu.VMEM((half, F_DEV), F32), dma((3,))],
        compiler_params=pltpu.CompilerParams(vmem_limit_bytes=8 * 2**20),
        name="finish",
    )(*parts)


def solution(mesh):
    return jax.shard_map(
        functools.partial(per_device, mesh.shape["fib"], mesh.shape["wav"]),
        mesh=mesh,
        in_specs=(
            P("exp", "wav", "fib"),
            P("exp", "wav", "fib"),
            P("exp", "wav", "fib"),
            P("fib"),
            P("fib"),
            P("exp", "fib"),
            P(),
        ),
        out_specs=(
            P(("wav", "exp"), "fib"),
            P(("wav", "exp"), "fib"),
            P(None, ("wav", "exp"), "fib"),
        ),
        check_vma=False,
    )
```

```python
import functools

import jax
import jax.numpy as jnp
from jax import lax
from jax.experimental import pallas as pl
from jax.experimental.pallas import tpu as pltpu
from jax.sharding import PartitionSpec as P

HALO = 50
BLOCKS = 8
BITS = 15
LANES = 128
HALVES = 2
F_DEV = LANES * HALVES
TILES = 2
ROWS = LANES * TILES
SLOT_ROW = 240
RING = 8

F32 = jnp.float32
BF16 = jnp.bfloat16


def pieces(x):
    high = x.astype(BF16)
    rest = x - high.astype(F32)
    middle = rest.astype(BF16)
    low = (rest - middle.astype(F32)).astype(BF16)
    return high, middle, low


def exact_dot(one_hot, x, dims, one_hot_first):
    total = None
    for piece in pieces(x):
        pair = (one_hot, piece) if one_hot_first else (piece, one_hot)
        part = lax.dot_general(*pair, (dims, ((), ())), preferred_element_type=F32)
        total = part if total is None else total + part
    return total


def offsets(n_fib):
    n_z = RING if n_fib % RING == 0 else n_fib
    n_y = n_fib // n_z

    def hops(o):
        return min(o[0], n_y - o[0]) + min(o[1], n_z - o[1])

    others = [(dy, dz) for dy in range(n_y) for dz in range(n_z) if dy or dz]
    return n_y, n_z, sorted(others, key=lambda o: -hops(o))


def placed_rows(place, got_ref, count):
    x = jnp.concatenate([got_ref[tile].T for tile in range(TILES)], axis=0)
    return exact_dot(place, x, ((1,), (0,)), False)[:count]


def exchange_kernel(
    n_fib,
    n_wav,
    pix_hbm,
    ivar_hbm,
    bits_hbm,
    coupling_hbm,
    counts_hbm,
    good_hbm,
    slots_hbm,
    place_ref,
    ivar_out,
    res_out,
    got_f,
    coupling_ref,
    counts_ref,
    good_ref,
    slots_ref,
    pix,
    ivar,
    bits,
    weight,
    fac_m,
    fac_y,
    fac_q,
    sums,
    give,
    take,
    send,
    got_w,
    got_t,
    sort_ref,
    edge_out,
    edge_in,
    red,
    far,
    small_sem,
    load_sem,
    edge_send,
    edge_recv,
    half_send,
    half_recv,
    own_send,
    own_recv,
):
    fib, wav, exp = lax.axis_index("fib"), lax.axis_index("wav"), lax.axis_index("exp")
    e_dev = good_ref.shape[0]
    chains = e_dev * HALVES
    waves = ivar.shape[1]
    step_count = waves // BLOCKS
    words = bits.shape[1] // BLOCKS
    half = waves // 2
    per = F_DEV // n_fib

    def to(**where):
        return {"device_id": where, "device_id_type": pl.DeviceIdType.MESH}

    n_y, n_z, others = offsets(n_fib)
    fib_y, fib_z = fib // n_z, lax.rem(fib, n_z)

    def fib_peer(k):
        dy, dz = others[k]
        return lax.rem(fib_y + dy, n_y) * n_z + lax.rem(fib_z + dz, n_z)

    def fib_from(k):
        dy, dz = others[k]
        return lax.rem(fib_y + n_y - dy, n_y) * n_z + lax.rem(fib_z + n_z - dz, n_z)

    wav_right = lax.rem(wav + 1, n_wav)
    wav_left = lax.rem(wav + n_wav - 1, n_wav)
    partner = 1 - exp

    small = [
        pltpu.make_async_copy(src, dst, small_sem.at[number])
        for number, (src, dst) in enumerate(
            (
                (slots_hbm, slots_ref),
                (coupling_hbm, coupling_ref),
                (counts_hbm, counts_ref),
                (good_hbm, good_ref),
            )
        )
    ]
    for copy in small:
        copy.start()
    loads = []

    def load(src, dst, rows, number):
        for chain in range(chains):
            e, h = chain // HALVES, chain % HALVES
            copy = pltpu.make_async_copy(
                src.at[e, :, pl.ds(h * LANES, LANES)], dst.at[chain], load_sem.at[number, chain]
            )
            copy.start()
            loads.append(copy)

    load(bits_hbm, bits, None, 0)
    load(ivar_hbm, ivar, None, 1)

    barrier = pltpu.get_barrier_semaphore()

    for k in range(n_fib - 1):
        pl.semaphore_signal(barrier, inc=1, **to(fib=fib_peer(k)))
    pl.semaphore_signal(barrier, inc=1, **to(exp=partner))
    pl.semaphore_signal(barrier, inc=1, **to(wav=wav_right))
    pl.semaphore_signal(barrier, inc=1, **to(wav=wav_left))

    load(pix_hbm, pix, None, 2)

    for copy in small:
        copy.wait()

    slot_row = jnp.concatenate(
        [slots_ref[pl.ds(fib * HALVES + h, 1), :] for h in range(HALVES)], axis=1
    )
    owner = slot_row // F_DEV
    owned = owner == lax.broadcasted_iota(jnp.int32, (n_fib, F_DEV), 0)
    before = lax.broadcasted_iota(jnp.int32, (F_DEV, F_DEV), 0) < lax.broadcasted_iota(
        jnp.int32, (F_DEV, F_DEV), 1
    )
    one, zero = jnp.ones((), F32), jnp.zeros((), F32)
    earlier = jnp.dot(
        jnp.where(owned, one, zero).astype(BF16),
        jnp.where(before, one, zero).astype(BF16),
        preferred_element_type=F32,
    )
    rank = jnp.sum(jnp.where(owned, earlier, zero), axis=0, keepdims=True)
    place = owner.astype(F32) * float(per) + rank
    row_of = lax.broadcasted_iota(jnp.int32, (F_DEV, F_DEV), 0).astype(F32)
    sort_ref[...] = jnp.where(row_of == place, one, zero).astype(BF16)
    slot_f32 = (slot_row - owner * F_DEV).astype(F32)

    c = [jnp.broadcast_to(coupling_ref[pl.ds(h, 1), :], (BLOCKS, LANES)) for h in range(HALVES)]
    sublane = lax.broadcasted_iota(jnp.int32, (BLOCKS, LANES), 0)
    at_first = jnp.where((sublane == 0) & (wav == 0), one, zero)
    at_last = jnp.where((sublane == BLOCKS - 1) & (wav == n_wav - 1), one, zero)
    link_first = [2.0 * c[h] - c[h] * at_first for h in range(HALVES)]
    link_last = [2.0 * c[h] - c[h] * at_last for h in range(HALVES)]

    usable = []
    for chain in range(chains):
        e, h = chain // HALVES, chain % HALVES
        observed = (exp * e_dev + e) < counts_ref[pl.ds(h, 1), :]
        good = good_ref[pl.ds(e, 1), pl.ds(h * LANES, LANES)]
        usable.append(jnp.where(observed, good, 0) * ((1 << BITS) - 1))
    usable = [jnp.broadcast_to(u, (BLOCKS, LANES)) for u in usable]

    for copy in loads[: 2 * chains]:
        copy.wait()

    def spread(i):
        return pl.ds(i, BLOCKS, stride=step_count)

    def word_steps(k, _):
        kept_words = [
            bits[chain, pl.ds(k, BLOCKS, stride=words), :] & usable[chain]
            for chain in range(chains)
        ]

        def weigh(j, _):
            i = k * BITS + j
            for h in range(HALVES):
                w_sum = None
                for e in range(e_dev):
                    chain = e * HALVES + h
                    bit = (kept_words[chain] >> j) & 1
                    w = jnp.where(bit == 1, ivar[chain, spread(i), :], 0.0)
                    weight[i, chain] = w
                    w_sum = w if w_sum is None else w_sum + w
                sums[0, h, spread(i), :] = w_sum
            return 0

        return lax.fori_loop(0, BITS, weigh, 0, unroll=5)

    lax.fori_loop(0, words, word_steps, 0)

    pad = ROWS - half
    blank = jnp.zeros((pad, F_DEV), F32)
    slot_rows = jnp.where(
        lax.broadcasted_iota(jnp.int32, (pad, F_DEV), 0) == SLOT_ROW - half,
        jnp.broadcast_to(slot_f32, (pad, F_DEV)),
        blank,
    )
    my_half = pl.ds(pl.multiple_of(exp * half, 8), half)
    other_half = pl.ds(pl.multiple_of(partner * half, 8), half)

    def sort(number, rows, extra, dst):
        x = jnp.concatenate([sums[number, h, rows, :] for h in range(HALVES)], axis=1)
        x = jnp.concatenate([x, extra], axis=0)
        x = exact_dot(sort_ref[...], x, ((1,), (1,)), True)
        for tile in range(TILES):
            dst[number, tile] = x[:, tile * LANES : (tile + 1) * LANES]

    def give_copy(number, tile):
        return pltpu.make_async_remote_copy(
            give.at[number, tile],
            take.at[number, tile],
            half_send.at[number, tile],
            half_recv.at[number, tile],
            **to(exp=partner),
        )

    def give_all(number):
        for tile in range(TILES):
            give_copy(number, tile).start()
        sort(number, my_half, slot_rows if number == 0 else blank, send)

    got = (got_w, got_t, got_f)
    mine = pl.ds(pl.multiple_of(fib * per, 8), per)

    def owner_copy(number, k, source):
        p = pl.ds(pl.multiple_of(fib_peer(k) * per, 8), per)
        q = pl.ds(pl.multiple_of(source * per, 8), per)
        return pltpu.make_async_remote_copy(
            send.at[number, :, p, :],
            got[number].at[:, q, :],
            own_send.at[number, k],
            own_recv.at[number, k],
            **to(fib=fib_peer(k)),
        )

    def send_all(number):
        for tile in range(TILES):
            give_copy(number, tile).wait()
            send[number, tile] = send[number, tile] + take[number, tile]
            got[number][tile, mine, :] = send[number, tile, mine, :]
        for k in range(n_fib - 1):
            owner_copy(number, k, fib).start()

    def wait_all(number):
        for k in range(n_fib - 1):
            owner_copy(number, k, fib_from(k)).wait()

    sort(0, other_half, blank, give)
    pl.semaphore_wait(barrier, n_fib + 2)
    give_all(0)

    def band_step(i, _):
        first = jnp.where(i == 0, 1.0, 0.0)
        last = jnp.where(i == step_count - 1, 1.0, 0.0)
        for h in range(HALVES):
            both = 4.0 * c[h] - 2.0 * c[h] * (at_first * first + at_last * last)
            band = None
            for e in range(e_dev):
                chain = e * HALVES + h
                part = weight[i, chain] / (ivar[chain, spread(i), :] + both)
                band = part if band is None else band + part
            sums[1, h, spread(i), :] = band * c[h]
        return 0

    lax.fori_loop(0, step_count, band_step, 0)
    send_all(0)
    sort(1, other_half, blank, give)
    give_all(1)

    for copy in loads[2 * chains :]:
        copy.wait()

    c_e = [c[h][:e_dev] for h in range(HALVES)]

    def edge_row(ref, h, row):
        return jnp.concatenate(
            [ref[e * HALVES + h, pl.ds(row, 1), :] for e in range(e_dev)], axis=0
        )

    def edge_step(j, state):
        out = []
        for side in range(2):
            for h in range(HALVES):
                d, y = state[side * HALVES + h]
                row = waves - HALO + j if side == 0 else HALO - 1 - j
                iv, px = edge_row(ivar, h, row), edge_row(pix, h, row)
                m = c_e[h] / d
                out.append((iv + 2.0 * c_e[h] - c_e[h] * m, iv * px + m * y))
        return tuple(out)

    start = []
    for side in range(2):
        for h in range(HALVES):
            row = waves - HALO if side == 0 else HALO - 1
            iv, px = edge_row(ivar, h, row), edge_row(pix, h, row)
            start.append((iv + c_e[h], iv * px))
    ends = lax.fori_loop(1, HALO, edge_step, tuple(start))
    for side in range(2):
        for h in range(HALVES):
            for q in range(2):
                edge_out[side, q, pl.ds(h, e_dev, stride=HALVES), :] = ends[side * HALVES + h][q]

    def edge_copy(side):
        return pltpu.make_async_remote_copy(
            edge_out.at[side],
            edge_in.at[side],
            edge_send.at[side],
            edge_recv.at[side],
            **to(wav=wav_right if side == 0 else wav_left),
        )

    edges = [edge_copy(0), edge_copy(1)]
    for copy in edges:
        copy.start()
    send_all(1)

    def eliminate(i, link, state):
        out = []
        for chain in range(chains):
            h = chain % HALVES
            m, y, s, g, hh = state[chain]
            iv = ivar[chain, spread(i), :]
            b = iv * pix[chain, spread(i), :]
            d = iv + link[h] - c[h] * m
            y = b + m * y
            s = m * s if s is not None else c[h]
            r = 1.0 / d
            m = c[h] * r
            q = s * r
            g = g + q * s
            hh = hh + q * y
            fac_m[i, chain] = m
            fac_y[i, chain] = r * y
            fac_q[i, chain] = q
            out.append((m, y, s, g, hh))
        return tuple(out)

    nothing = jnp.zeros((BLOCKS, LANES), F32)
    state = eliminate(0, link_first, tuple((nothing, nothing, None, nothing, nothing) for _ in range(chains)))
    link_inner = [2.0 * c[h] for h in range(HALVES)]
    last = step_count - 1
    state = lax.fori_loop(1, last, lambda i, st: eliminate(i, link_inner, st), state)

    for chain in range(chains):
        h = chain % HALVES
        m, y, s, g, hh = state[chain]
        iv = ivar[chain, spread(last), :]
        b = iv * pix[chain, spread(last), :]
        rows = pl.ds(chain * BLOCKS, BLOCKS)
        red[0, rows, :] = iv + link_last[h] - c[h] * m
        red[1, rows, :] = b + m * y
        red[2, rows, :] = g
        red[3, rows, :] = hh
        red[4, rows, :] = c[h] * fac_q[last - 1, chain]
        red[5, pl.ds(chain, 1), :] = coupling_ref[pl.ds(h, 1), :]

    for copy in edges:
        copy.wait()

    def across(k, b):
        return red[k, pl.ds(b, chains, stride=BLOCKS), :]

    d_l, y_l = edge_in[0, 0], edge_in[0, 1]
    d_r, y_r = edge_in[1, 0], edge_in[1, 1]
    c_all = red[5, pl.ds(0, chains), :]
    e_b = [across(4, b) for b in range(BLOCKS)]
    d_b, z_b = [], []
    right = c_all / d_r
    for b in range(BLOCKS):
        if b + 1 < BLOCKS:
            g_next, h_next = across(2, b + 1), across(3, b + 1)
        else:
            g_next = jnp.where(wav < n_wav - 1, c_all * right, 0.0)
            h_next = jnp.where(wav < n_wav - 1, y_r * right, 0.0)
        d_b.append(across(0, b) - g_next)
        z_b.append(across(1, b) + h_next)
    r_l = jnp.where(wav > 0, 1.0 / (d_l - across(2, 0)), 0.0)
    p_l = jnp.where(wav > 0, y_l + across(3, 0), 0.0)
    prev_e = e_b[0] * r_l
    d_b[0] = d_b[0] - e_b[0] * prev_e
    z_b[0] = z_b[0] + p_l * prev_e
    inv = []
    for b in range(BLOCKS):
        inv.append(1.0 / d_b[b])
        if b + 1 < BLOCKS:
            prev_e = e_b[b + 1] * inv[b]
            d_b[b + 1] = d_b[b + 1] - e_b[b + 1] * prev_e
            z_b[b + 1] = z_b[b + 1] + z_b[b] * prev_e
    x = None
    for b in reversed(range(BLOCKS)):
        x = inv[b] * (z_b[b] if x is None else z_b[b] + e_b[b + 1] * x)
        far[0, pl.ds(b, chains, stride=BLOCKS), :] = x
        if b + 1 < BLOCKS:
            far[1, pl.ds(b + 1, chains, stride=BLOCKS), :] = x
    far[1, pl.ds(0, chains, stride=BLOCKS), :] = r_l * (p_l + e_b[0] * x)

    def flux_at(i, xs):
        for h in range(HALVES):
            total = None
            for e in range(e_dev):
                chain = e * HALVES + h
                part = weight[i, chain] * xs[chain]
                total = part if total is None else total + part
            sums[2, h, spread(i), :] = total

    xs = [far[0, pl.ds(chain * BLOCKS, BLOCKS), :] for chain in range(chains)]
    lefts = [far[1, pl.ds(chain * BLOCKS, BLOCKS), :] for chain in range(chains)]
    flux_at(last, xs)

    def substitute(k, xs):
        i = last - 1 - k
        xs = tuple(
            fac_y[i, chain] + fac_q[i, chain] * lefts[chain] + fac_m[i, chain] * xs[chain]
            for chain in range(chains)
        )
        flux_at(i, xs)
        return xs

    lax.fori_loop(0, last, substitute, tuple(xs))

    sort(2, other_half, blank, give)
    give_all(2)
    send_all(2)

    wait_all(0)
    slot = got_w[SLOT_ROW // LANES, :, pl.ds(SLOT_ROW % LANES, 1)]
    lane = lax.broadcasted_iota(jnp.int32, (F_DEV, F_DEV), 1).astype(F32)
    place_ref[...] = jnp.where(slot == lane, one, zero).astype(BF16)
    place = place_ref[...]
    ivar_out[...] = placed_rows(place, got_w, half)
    wait_all(1)
    band = placed_rows(place, got_t, half)
    weight_sum = ivar_out[...]
    row = lax.broadcasted_iota(jnp.int32, (half, F_DEV), 0)
    lower = jnp.where((row == 0) & (wav == 0) & (exp == 0), 0.0, band)
    upper = jnp.where((row == half - 1) & (wav == n_wav - 1) & (exp == 1), 0.0, band)
    divisor = jnp.maximum(weight_sum, 1.0)
    res_out[0] = lower / divisor
    res_out[1] = (weight_sum - lower - upper) / divisor
    res_out[2] = upper / divisor
    wait_all(2)


def finish_kernel(place_ref, ivar_ref, res_ref, got_ref, flux_hbm, ivar_hbm, res_hbm, flux, sems):
    half = ivar_ref.shape[0]
    copies = [
        pltpu.make_async_copy(ivar_ref, ivar_hbm, sems.at[0]),
        pltpu.make_async_copy(res_ref, res_hbm, sems.at[1]),
        pltpu.make_async_copy(flux, flux_hbm, sems.at[2]),
    ]
    copies[0].start()
    copies[1].start()
    flux[...] = placed_rows(place_ref[...], got_ref, half) / jnp.maximum(ivar_ref[...], 1.0)
    copies[2].start()
    for copy in copies:
        copy.wait()


def per_device(n_fib, n_wav, pixels, pixel_ivar, clip_bits, coupling, counts, good_flags, owner_slot):
    e_dev, waves, _ = pixels.shape
    n_words = clip_bits.shape[1]
    chains = e_dev * HALVES
    steps = waves // BLOCKS
    half = waves // 2
    vmem = pl.BlockSpec(memory_space=pltpu.VMEM)
    hbm = pl.BlockSpec(memory_space=pltpu.HBM)
    dma = pltpu.SemaphoreType.DMA
    limit = 24 * 2**20
    parts = pl.pallas_call(
        functools.partial(exchange_kernel, n_fib, n_wav),
        out_shape=(
            jax.ShapeDtypeStruct((F_DEV, F_DEV), BF16),
            jax.ShapeDtypeStruct((half, F_DEV), F32),
            jax.ShapeDtypeStruct((3, half, F_DEV), F32),
            jax.ShapeDtypeStruct((TILES, F_DEV, LANES), F32),
        ),
        in_specs=[hbm] * 7,
        out_specs=(vmem,) * 4,
        scratch_shapes=[
            pltpu.VMEM((HALVES, LANES), F32),
            pltpu.VMEM((HALVES, LANES), jnp.int32),
            pltpu.VMEM(good_flags.shape, jnp.int32),
            pltpu.VMEM((owner_slot.shape[0] // LANES, LANES), jnp.int32),
            pltpu.VMEM((chains, waves, LANES), F32),
            pltpu.VMEM((chains, waves, LANES), F32),
            pltpu.VMEM((chains, n_words, LANES), jnp.int32),
            pltpu.VMEM((steps, chains, BLOCKS, LANES), F32),
            pltpu.VMEM((steps, chains, BLOCKS, LANES), F32),
            pltpu.VMEM((steps, chains, BLOCKS, LANES), F32),
            pltpu.VMEM((steps, chains, BLOCKS, LANES), F32),
            pltpu.VMEM((3, HALVES, waves, LANES), F32),
            pltpu.VMEM((3, TILES, F_DEV, LANES), F32),
            pltpu.VMEM((3, TILES, F_DEV, LANES), F32),
            pltpu.VMEM((3, TILES, F_DEV, LANES), F32),
            pltpu.VMEM((TILES, F_DEV, LANES), F32),
            pltpu.VMEM((TILES, F_DEV, LANES), F32),
            pltpu.VMEM((F_DEV, F_DEV), BF16),
            pltpu.VMEM((2, 2, chains, LANES), F32),
            pltpu.VMEM((2, 2, chains, LANES), F32),
            pltpu.VMEM((6, chains * BLOCKS, LANES), F32),
            pltpu.VMEM((2, chains * BLOCKS, LANES), F32),
            dma((4,)),
            dma((3, chains)),
            dma((2,)),
            dma((2,)),
            dma((3, TILES)),
            dma((3, TILES)),
            dma((3, n_fib - 1)),
            dma((3, n_fib - 1)),
        ],
        compiler_params=pltpu.CompilerParams(
            collective_id=0, has_side_effects=True, vmem_limit_bytes=limit
        ),
        name="exchange",
    )(
        *(
            pltpu.with_memory_space_constraint(x, pltpu.HBM)
            for x in (
                pixels,
                pixel_ivar,
                clip_bits,
                coupling.reshape(HALVES, LANES),
                counts.reshape(HALVES, LANES),
                good_flags,
                owner_slot.reshape(-1, LANES),
            )
        )
    )
    return pl.pallas_call(
        finish_kernel,
        out_shape=(
            jax.ShapeDtypeStruct((half, F_DEV), F32),
            jax.ShapeDtypeStruct((half, F_DEV), F32),
            jax.ShapeDtypeStruct((3, half, F_DEV), F32),
        ),
        in_specs=[vmem] * 4,
        out_specs=(hbm,) * 3,
        scratch_shapes=[pltpu.VMEM((half, F_DEV), F32), dma((3,))],
        compiler_params=pltpu.CompilerParams(vmem_limit_bytes=8 * 2**20),
        name="finish",
    )(*parts)


def solution(mesh):
    return jax.shard_map(
        functools.partial(per_device, mesh.shape["fib"], mesh.shape["wav"]),
        mesh=mesh,
        in_specs=(
            P("exp", "wav", "fib"),
            P("exp", "wav", "fib"),
            P("exp", "wav", "fib"),
            P("fib"),
            P("fib"),
            P("exp", "fib"),
            P(),
        ),
        out_specs=(
            P(("wav", "exp"), "fib"),
            P(("wav", "exp"), "fib"),
            P(None, ("wav", "exp"), "fib"),
        ),
        check_vma=False,
    )
```

```python
import functools

import jax
import jax.numpy as jnp
from jax import lax
from jax.experimental import pallas as pl
from jax.experimental.pallas import tpu as pltpu
from jax.sharding import PartitionSpec as P

HALO = 50
BLOCKS = 8
BITS = 15
LANES = 128
HALVES = 2
F_DEV = LANES * HALVES
TILES = 2
ROWS = LANES * TILES
SLOT_ROW = 240
RING = 8

F32 = jnp.float32
BF16 = jnp.bfloat16


def pieces(x):
    high = x.astype(BF16)
    rest = x - high.astype(F32)
    middle = rest.astype(BF16)
    low = (rest - middle.astype(F32)).astype(BF16)
    return high, middle, low


def exact_dot(one_hot, x, dims, one_hot_first):
    total = None
    for piece in pieces(x):
        pair = (one_hot, piece) if one_hot_first else (piece, one_hot)
        part = lax.dot_general(*pair, (dims, ((), ())), preferred_element_type=F32)
        total = part if total is None else total + part
    return total


def offsets(n_fib):
    n_z = RING if n_fib % RING == 0 else n_fib
    n_y = n_fib // n_z

    def hops(o):
        return min(o[0], n_y - o[0]) + min(o[1], n_z - o[1])

    others = [(dy, dz) for dy in range(n_y) for dz in range(n_z) if dy or dz]
    return n_y, n_z, sorted(others, key=lambda o: -hops(o))


def placed_rows(place, got_ref, count):
    x = jnp.concatenate([got_ref[tile].T for tile in range(TILES)], axis=0)
    return exact_dot(place, x, ((1,), (0,)), False)[:count]


def exchange_kernel(
    n_fib,
    n_wav,
    pix_hbm,
    ivar_hbm,
    bits_hbm,
    coupling_hbm,
    counts_hbm,
    good_hbm,
    slots_hbm,
    place_ref,
    ivar_out,
    res_out,
    got_f,
    coupling_ref,
    counts_ref,
    good_ref,
    slots_ref,
    pix,
    ivar,
    bits,
    weight,
    fac_m,
    fac_y,
    fac_q,
    sums,
    give,
    take,
    send,
    got_w,
    got_t,
    sort_ref,
    edge_out,
    edge_in,
    red,
    far,
    small_sem,
    load_sem,
    edge_send,
    edge_recv,
    half_send,
    half_recv,
    own_send,
    own_recv,
):
    fib, wav, exp = lax.axis_index("fib"), lax.axis_index("wav"), lax.axis_index("exp")
    e_dev = good_ref.shape[0]
    chains = e_dev * HALVES
    waves = ivar.shape[1]
    step_count = waves // BLOCKS
    words = bits.shape[1] // BLOCKS
    half = waves // 2
    per = F_DEV // n_fib

    def to(**where):
        return {"device_id": where, "device_id_type": pl.DeviceIdType.MESH}

    n_y, n_z, others = offsets(n_fib)
    fib_y, fib_z = fib // n_z, lax.rem(fib, n_z)

    def fib_peer(k):
        dy, dz = others[k]
        return lax.rem(fib_y + dy, n_y) * n_z + lax.rem(fib_z + dz, n_z)

    def fib_from(k):
        dy, dz = others[k]
        return lax.rem(fib_y + n_y - dy, n_y) * n_z + lax.rem(fib_z + n_z - dz, n_z)

    wav_right = lax.rem(wav + 1, n_wav)
    wav_left = lax.rem(wav + n_wav - 1, n_wav)
    partner = 1 - exp

    small = [
        pltpu.make_async_copy(src, dst, small_sem.at[number])
        for number, (src, dst) in enumerate(
            (
                (slots_hbm, slots_ref),
                (coupling_hbm, coupling_ref),
                (counts_hbm, counts_ref),
                (good_hbm, good_ref),
            )
        )
    ]
    for copy in small:
        copy.start()
    loads = []

    def load(src, dst, rows, number):
        for chain in range(chains):
            e, h = chain // HALVES, chain % HALVES
            copy = pltpu.make_async_copy(
                src.at[e, :, pl.ds(h * LANES, LANES)], dst.at[chain], load_sem.at[number, chain]
            )
            copy.start()
            loads.append(copy)

    load(bits_hbm, bits, None, 0)
    load(ivar_hbm, ivar, None, 1)

    barrier = pltpu.get_barrier_semaphore()

    for k in range(n_fib - 1):
        pl.semaphore_signal(barrier, inc=1, **to(fib=fib_peer(k)))
    pl.semaphore_signal(barrier, inc=1, **to(exp=partner))
    pl.semaphore_signal(barrier, inc=1, **to(wav=wav_right))
    pl.semaphore_signal(barrier, inc=1, **to(wav=wav_left))

    load(pix_hbm, pix, None, 2)

    for copy in small:
        copy.wait()

    slot_row = jnp.concatenate(
        [slots_ref[pl.ds(fib * HALVES + h, 1), :] for h in range(HALVES)], axis=1
    )
    owner = slot_row // F_DEV
    owned = owner == lax.broadcasted_iota(jnp.int32, (n_fib, F_DEV), 0)
    before = lax.broadcasted_iota(jnp.int32, (F_DEV, F_DEV), 0) < lax.broadcasted_iota(
        jnp.int32, (F_DEV, F_DEV), 1
    )
    one, zero = jnp.ones((), F32), jnp.zeros((), F32)
    earlier = jnp.dot(
        jnp.where(owned, one, zero).astype(BF16),
        jnp.where(before, one, zero).astype(BF16),
        preferred_element_type=F32,
    )
    rank = jnp.sum(jnp.where(owned, earlier, zero), axis=0, keepdims=True)
    place = owner.astype(F32) * float(per) + rank
    row_of = lax.broadcasted_iota(jnp.int32, (F_DEV, F_DEV), 0).astype(F32)
    sort_ref[...] = jnp.where(row_of == place, one, zero).astype(BF16)
    slot_f32 = (slot_row - owner * F_DEV).astype(F32)

    c = [jnp.broadcast_to(coupling_ref[pl.ds(h, 1), :], (BLOCKS, LANES)) for h in range(HALVES)]
    sublane = lax.broadcasted_iota(jnp.int32, (BLOCKS, LANES), 0)
    at_first = jnp.where((sublane == 0) & (wav == 0), one, zero)
    at_last = jnp.where((sublane == BLOCKS - 1) & (wav == n_wav - 1), one, zero)
    link_first = [2.0 * c[h] - c[h] * at_first for h in range(HALVES)]
    link_last = [2.0 * c[h] - c[h] * at_last for h in range(HALVES)]

    usable = []
    for chain in range(chains):
        e, h = chain // HALVES, chain % HALVES
        observed = (exp * e_dev + e) < counts_ref[pl.ds(h, 1), :]
        good = good_ref[pl.ds(e, 1), pl.ds(h * LANES, LANES)]
        usable.append(jnp.where(observed, good, 0) * ((1 << BITS) - 1))
    usable = [jnp.broadcast_to(u, (BLOCKS, LANES)) for u in usable]

    for copy in loads[: 2 * chains]:
        copy.wait()

    def spread(i):
        return pl.ds(i, BLOCKS, stride=step_count)

    def word_steps(k, _):
        kept_words = [
            bits[chain, pl.ds(k, BLOCKS, stride=words), :] & usable[chain]
            for chain in range(chains)
        ]

        def weigh(j, _):
            i = k * BITS + j
            for h in range(HALVES):
                w_sum = None
                for e in range(e_dev):
                    chain = e * HALVES + h
                    bit = (kept_words[chain] >> j) & 1
                    w = jnp.where(bit == 1, ivar[chain, spread(i), :], 0.0)
                    weight[i, chain] = w
                    w_sum = w if w_sum is None else w_sum + w
                sums[0, h, spread(i), :] = w_sum
            return 0

        return lax.fori_loop(0, BITS, weigh, 0, unroll=5)

    lax.fori_loop(0, words, word_steps, 0)

    pad = ROWS - half
    blank = jnp.zeros((pad, F_DEV), F32)
    slot_rows = jnp.where(
        lax.broadcasted_iota(jnp.int32, (pad, F_DEV), 0) == SLOT_ROW - half,
        jnp.broadcast_to(slot_f32, (pad, F_DEV)),
        blank,
    )
    my_half = pl.ds(pl.multiple_of(exp * half, 8), half)
    other_half = pl.ds(pl.multiple_of(partner * half, 8), half)

    def sort(number, rows, extra, dst):
        x = jnp.concatenate([sums[number, h, rows, :] for h in range(HALVES)], axis=1)
        x = jnp.concatenate([x, extra], axis=0)
        x = exact_dot(sort_ref[...], x, ((1,), (1,)), True)
        for tile in range(TILES):
            dst[number, tile] = x[:, tile * LANES : (tile + 1) * LANES]

    def give_copy(number, tile):
        return pltpu.make_async_remote_copy(
            give.at[number, tile],
            take.at[number, tile],
            half_send.at[number, tile],
            half_recv.at[number, tile],
            **to(exp=partner),
        )

    def give_all(number):
        for tile in range(TILES):
            give_copy(number, tile).start()
        sort(number, my_half, slot_rows if number == 0 else blank, send)

    got = (got_w, got_t, got_f)
    mine = pl.ds(pl.multiple_of(fib * per, 8), per)

    def tile_copy(number, k, tile):
        p = pl.ds(pl.multiple_of(fib_peer(k) * per, 8), per)
        return pltpu.make_async_remote_copy(
            send.at[number, tile, p, :],
            got[number].at[tile, mine, :],
            own_send.at[number, k],
            own_recv.at[number, k],
            **to(fib=fib_peer(k)),
        )

    def owner_copy(number, k, source):
        p = pl.ds(pl.multiple_of(fib_peer(k) * per, 8), per)
        q = pl.ds(pl.multiple_of(source * per, 8), per)
        return pltpu.make_async_remote_copy(
            send.at[number, :, p, :],
            got[number].at[:, q, :],
            own_send.at[number, k],
            own_recv.at[number, k],
            **to(fib=fib_peer(k)),
        )

    def send_all(number):
        for tile in range(TILES):
            give_copy(number, tile).wait()
            send[number, tile] = send[number, tile] + take[number, tile]
            got[number][tile, mine, :] = send[number, tile, mine, :]
            for k in range(n_fib - 1):
                tile_copy(number, k, tile).start()

    def wait_all(number):
        for k in range(n_fib - 1):
            owner_copy(number, k, fib_from(k)).wait()

    sort(0, other_half, blank, give)
    pl.semaphore_wait(barrier, n_fib + 2)
    give_all(0)

    send_all(0)
    def band_step(i, _):
        first = jnp.where(i == 0, 1.0, 0.0)
        last = jnp.where(i == step_count - 1, 1.0, 0.0)
        for h in range(HALVES):
            both = 4.0 * c[h] - 2.0 * c[h] * (at_first * first + at_last * last)
            band = None
            for e in range(e_dev):
                chain = e * HALVES + h
                part = weight[i, chain] / (ivar[chain, spread(i), :] + both)
                band = part if band is None else band + part
            sums[1, h, spread(i), :] = band * c[h]
        return 0

    lax.fori_loop(0, step_count, band_step, 0)
    sort(1, other_half, blank, give)
    give_all(1)

    for copy in loads[2 * chains :]:
        copy.wait()

    c_e = [c[h][:e_dev] for h in range(HALVES)]

    def edge_row(ref, h, row):
        return jnp.concatenate(
            [ref[e * HALVES + h, pl.ds(row, 1), :] for e in range(e_dev)], axis=0
        )

    def edge_step(j, state):
        out = []
        for side in range(2):
            for h in range(HALVES):
                d, y = state[side * HALVES + h]
                row = waves - HALO + j if side == 0 else HALO - 1 - j
                iv, px = edge_row(ivar, h, row), edge_row(pix, h, row)
                m = c_e[h] / d
                out.append((iv + 2.0 * c_e[h] - c_e[h] * m, iv * px + m * y))
        return tuple(out)

    start = []
    for side in range(2):
        for h in range(HALVES):
            row = waves - HALO if side == 0 else HALO - 1
            iv, px = edge_row(ivar, h, row), edge_row(pix, h, row)
            start.append((iv + c_e[h], iv * px))
    ends = lax.fori_loop(1, HALO, edge_step, tuple(start))
    for side in range(2):
        for h in range(HALVES):
            for q in range(2):
                edge_out[side, q, pl.ds(h, e_dev, stride=HALVES), :] = ends[side * HALVES + h][q]

    def edge_copy(side):
        return pltpu.make_async_remote_copy(
            edge_out.at[side],
            edge_in.at[side],
            edge_send.at[side],
            edge_recv.at[side],
            **to(wav=wav_right if side == 0 else wav_left),
        )

    edges = [edge_copy(0), edge_copy(1)]
    for copy in edges:
        copy.start()
    send_all(1)

    def eliminate(i, link, state):
        out = []
        for chain in range(chains):
            h = chain % HALVES
            m, y, s, g, hh = state[chain]
            iv = ivar[chain, spread(i), :]
            b = iv * pix[chain, spread(i), :]
            d = iv + link[h] - c[h] * m
            y = b + m * y
            s = m * s if s is not None else c[h]
            r = 1.0 / d
            m = c[h] * r
            q = s * r
            g = g + q * s
            hh = hh + q * y
            fac_m[i, chain] = m
            fac_y[i, chain] = r * y
            fac_q[i, chain] = q
            out.append((m, y, s, g, hh))
        return tuple(out)

    nothing = jnp.zeros((BLOCKS, LANES), F32)
    state = eliminate(0, link_first, tuple((nothing, nothing, None, nothing, nothing) for _ in range(chains)))
    link_inner = [2.0 * c[h] for h in range(HALVES)]
    last = step_count - 1
    state = lax.fori_loop(1, last, lambda i, st: eliminate(i, link_inner, st), state)

    for chain in range(chains):
        h = chain % HALVES
        m, y, s, g, hh = state[chain]
        iv = ivar[chain, spread(last), :]
        b = iv * pix[chain, spread(last), :]
        rows = pl.ds(chain * BLOCKS, BLOCKS)
        red[0, rows, :] = iv + link_last[h] - c[h] * m
        red[1, rows, :] = b + m * y
        red[2, rows, :] = g
        red[3, rows, :] = hh
        red[4, rows, :] = c[h] * fac_q[last - 1, chain]
        red[5, pl.ds(chain, 1), :] = coupling_ref[pl.ds(h, 1), :]

    for copy in edges:
        copy.wait()

    def across(k, b):
        return red[k, pl.ds(b, chains, stride=BLOCKS), :]

    d_l, y_l = edge_in[0, 0], edge_in[0, 1]
    d_r, y_r = edge_in[1, 0], edge_in[1, 1]
    c_all = red[5, pl.ds(0, chains), :]
    e_b = [across(4, b) for b in range(BLOCKS)]
    d_b, z_b = [], []
    right = c_all / d_r
    for b in range(BLOCKS):
        if b + 1 < BLOCKS:
            g_next, h_next = across(2, b + 1), across(3, b + 1)
        else:
            g_next = jnp.where(wav < n_wav - 1, c_all * right, 0.0)
            h_next = jnp.where(wav < n_wav - 1, y_r * right, 0.0)
        d_b.append(across(0, b) - g_next)
        z_b.append(across(1, b) + h_next)
    r_l = jnp.where(wav > 0, 1.0 / (d_l - across(2, 0)), 0.0)
    p_l = jnp.where(wav > 0, y_l + across(3, 0), 0.0)
    prev_e = e_b[0] * r_l
    d_b[0] = d_b[0] - e_b[0] * prev_e
    z_b[0] = z_b[0] + p_l * prev_e
    inv = []
    for b in range(BLOCKS):
        inv.append(1.0 / d_b[b])
        if b + 1 < BLOCKS:
            prev_e = e_b[b + 1] * inv[b]
            d_b[b + 1] = d_b[b + 1] - e_b[b + 1] * prev_e
            z_b[b + 1] = z_b[b + 1] + z_b[b] * prev_e
    x = None
    for b in reversed(range(BLOCKS)):
        x = inv[b] * (z_b[b] if x is None else z_b[b] + e_b[b + 1] * x)
        far[0, pl.ds(b, chains, stride=BLOCKS), :] = x
        if b + 1 < BLOCKS:
            far[1, pl.ds(b + 1, chains, stride=BLOCKS), :] = x
    far[1, pl.ds(0, chains, stride=BLOCKS), :] = r_l * (p_l + e_b[0] * x)

    def flux_at(i, xs):
        for h in range(HALVES):
            total = None
            for e in range(e_dev):
                chain = e * HALVES + h
                part = weight[i, chain] * xs[chain]
                total = part if total is None else total + part
            sums[2, h, spread(i), :] = total

    xs = [far[0, pl.ds(chain * BLOCKS, BLOCKS), :] for chain in range(chains)]
    lefts = [far[1, pl.ds(chain * BLOCKS, BLOCKS), :] for chain in range(chains)]
    flux_at(last, xs)

    def substitute(k, xs):
        i = last - 1 - k
        xs = tuple(
            fac_y[i, chain] + fac_q[i, chain] * lefts[chain] + fac_m[i, chain] * xs[chain]
            for chain in range(chains)
        )
        flux_at(i, xs)
        return xs

    lax.fori_loop(0, last, substitute, tuple(xs))

    sort(2, other_half, blank, give)
    give_all(2)
    send_all(2)

    wait_all(0)
    slot = got_w[SLOT_ROW // LANES, :, pl.ds(SLOT_ROW % LANES, 1)]
    lane = lax.broadcasted_iota(jnp.int32, (F_DEV, F_DEV), 1).astype(F32)
    place_ref[...] = jnp.where(slot == lane, one, zero).astype(BF16)
    place = place_ref[...]
    ivar_out[...] = placed_rows(place, got_w, half)
    wait_all(1)
    band = placed_rows(place, got_t, half)
    weight_sum = ivar_out[...]
    row = lax.broadcasted_iota(jnp.int32, (half, F_DEV), 0)
    lower = jnp.where((row == 0) & (wav == 0) & (exp == 0), 0.0, band)
    upper = jnp.where((row == half - 1) & (wav == n_wav - 1) & (exp == 1), 0.0, band)
    divisor = jnp.maximum(weight_sum, 1.0)
    res_out[0] = lower / divisor
    res_out[1] = (weight_sum - lower - upper) / divisor
    res_out[2] = upper / divisor
    wait_all(2)


def finish_kernel(place_ref, ivar_ref, res_ref, got_ref, flux_hbm, ivar_hbm, res_hbm, flux, sems):
    half = ivar_ref.shape[0]
    copies = [
        pltpu.make_async_copy(ivar_ref, ivar_hbm, sems.at[0]),
        pltpu.make_async_copy(res_ref, res_hbm, sems.at[1]),
        pltpu.make_async_copy(flux, flux_hbm, sems.at[2]),
    ]
    copies[0].start()
    copies[1].start()
    flux[...] = placed_rows(place_ref[...], got_ref, half) / jnp.maximum(ivar_ref[...], 1.0)
    copies[2].start()
    for copy in copies:
        copy.wait()


def per_device(n_fib, n_wav, pixels, pixel_ivar, clip_bits, coupling, counts, good_flags, owner_slot):
    e_dev, waves, _ = pixels.shape
    n_words = clip_bits.shape[1]
    chains = e_dev * HALVES
    steps = waves // BLOCKS
    half = waves // 2
    vmem = pl.BlockSpec(memory_space=pltpu.VMEM)
    hbm = pl.BlockSpec(memory_space=pltpu.HBM)
    dma = pltpu.SemaphoreType.DMA
    limit = 24 * 2**20
    parts = pl.pallas_call(
        functools.partial(exchange_kernel, n_fib, n_wav),
        out_shape=(
            jax.ShapeDtypeStruct((F_DEV, F_DEV), BF16),
            jax.ShapeDtypeStruct((half, F_DEV), F32),
            jax.ShapeDtypeStruct((3, half, F_DEV), F32),
            jax.ShapeDtypeStruct((TILES, F_DEV, LANES), F32),
        ),
        in_specs=[hbm] * 7,
        out_specs=(vmem,) * 4,
        scratch_shapes=[
            pltpu.VMEM((HALVES, LANES), F32),
            pltpu.VMEM((HALVES, LANES), jnp.int32),
            pltpu.VMEM(good_flags.shape, jnp.int32),
            pltpu.VMEM((owner_slot.shape[0] // LANES, LANES), jnp.int32),
            pltpu.VMEM((chains, waves, LANES), F32),
            pltpu.VMEM((chains, waves, LANES), F32),
            pltpu.VMEM((chains, n_words, LANES), jnp.int32),
            pltpu.VMEM((steps, chains, BLOCKS, LANES), F32),
            pltpu.VMEM((steps, chains, BLOCKS, LANES), F32),
            pltpu.VMEM((steps, chains, BLOCKS, LANES), F32),
            pltpu.VMEM((steps, chains, BLOCKS, LANES), F32),
            pltpu.VMEM((3, HALVES, waves, LANES), F32),
            pltpu.VMEM((3, TILES, F_DEV, LANES), F32),
            pltpu.VMEM((3, TILES, F_DEV, LANES), F32),
            pltpu.VMEM((3, TILES, F_DEV, LANES), F32),
            pltpu.VMEM((TILES, F_DEV, LANES), F32),
            pltpu.VMEM((TILES, F_DEV, LANES), F32),
            pltpu.VMEM((F_DEV, F_DEV), BF16),
            pltpu.VMEM((2, 2, chains, LANES), F32),
            pltpu.VMEM((2, 2, chains, LANES), F32),
            pltpu.VMEM((6, chains * BLOCKS, LANES), F32),
            pltpu.VMEM((2, chains * BLOCKS, LANES), F32),
            dma((4,)),
            dma((3, chains)),
            dma((2,)),
            dma((2,)),
            dma((3, TILES)),
            dma((3, TILES)),
            dma((3, n_fib - 1)),
            dma((3, n_fib - 1)),
        ],
        compiler_params=pltpu.CompilerParams(
            collective_id=0, has_side_effects=True, vmem_limit_bytes=limit
        ),
        name="exchange",
    )(
        *(
            pltpu.with_memory_space_constraint(x, pltpu.HBM)
            for x in (
                pixels,
                pixel_ivar,
                clip_bits,
                coupling.reshape(HALVES, LANES),
                counts.reshape(HALVES, LANES),
                good_flags,
                owner_slot.reshape(-1, LANES),
            )
        )
    )
    return pl.pallas_call(
        finish_kernel,
        out_shape=(
            jax.ShapeDtypeStruct((half, F_DEV), F32),
            jax.ShapeDtypeStruct((half, F_DEV), F32),
            jax.ShapeDtypeStruct((3, half, F_DEV), F32),
        ),
        in_specs=[vmem] * 4,
        out_specs=(hbm,) * 3,
        scratch_shapes=[pltpu.VMEM((half, F_DEV), F32), dma((3,))],
        compiler_params=pltpu.CompilerParams(vmem_limit_bytes=8 * 2**20),
        name="finish",
    )(*parts)


def solution(mesh):
    return jax.shard_map(
        functools.partial(per_device, mesh.shape["fib"], mesh.shape["wav"]),
        mesh=mesh,
        in_specs=(
            P("exp", "wav", "fib"),
            P("exp", "wav", "fib"),
            P("exp", "wav", "fib"),
            P("fib"),
            P("fib"),
            P("exp", "fib"),
            P(),
        ),
        out_specs=(
            P(("wav", "exp"), "fib"),
            P(("wav", "exp"), "fib"),
            P(None, ("wav", "exp"), "fib"),
        ),
        check_vma=False,
    )
```
